32 devices in a mesh: space: 8 (over z, y), samp: 4 (over x, core).
Axes of the slice: x: 2, y: 2, z: 4, core: 2. Of those that a mesh axis runs over, the one named last changes fastest.
Arguments:
- volume: bfloat16 [4, 32, 32, 256], P(None, 'space', 'samp'), may hold values from -6 to 6
- filters_one: bfloat16 [1728], P('samp'), may hold values from -0.625 to 0.625
- filters_two: bfloat16 [13824], P('space'), may hold values from -0.3125 to 0.3125
- cotangent: bfloat16 [32, 32, 32, 256], P(None, 'space', 'samp'), may hold values from -6 to 6
Outputs:
- activation: bfloat16 [32, 32, 32, 256], P(None, 'space', 'samp')
- grad_one: float32 [1728], P('samp')
- grad_two: float32 [13824], P('space')
The draws below stay inside these ranges and needn't reach their ends.
All inputs are finite; a program needn't handle non-finite values.
Results may differ from the reference program's by a relative error of at most 0.0044.
The reference program's roundings to bfloat16 on the way count: a program that leaves them out, or rounds other values in their place, can miss the bound.
Values may be sent and summed in bfloat16 or wider, within the bound.
A program may use at most 64 MiB of HBM per device.

```python
import math
import jax
import jax.numpy as jnp
from jax import lax

CIN = 4
C1 = 16
C2 = 32
CZ = 256
NX = 32
NY = 32


def shard_levels(key, shape, cuts, least, top_value):
    factor_of = 1.0
    for position, blocks in cuts:
        heights = jax.random.uniform(jax.random.fold_in(jax.random.fold_in(key, 6), position), (blocks,), jnp.float32, least / len(cuts), top_value / len(cuts))
        factor_of = factor_of * jnp.repeat(jnp.exp(heights), shape[position] // blocks).reshape((-1,) + (1,) * (len(shape) - 1 - position))
    return factor_of


def noise(stream_key, dims, spread, bound, shards=(), dtype=jnp.bfloat16):
    values = jax.random.normal(stream_key, dims, jnp.float32) * spread
    if len(shards) > 0:
        values = shard_levels(stream_key, dims, shards, -0.22, 0.18) * values
    return jnp.clip(values, min=-bound, max=bound).astype(dtype)


def setup_inputs(seed: int = 0) -> dict:
    arg_keys = jax.random.split(jax.random.key(seed), 5)
    volume = noise(arg_keys[0], (CIN, NX, NY, CZ), 1.0, 6.0, ((1, 8), (2, 4)))
    filters_one = noise(arg_keys[1], (27 * CIN * C1,), (27 * CIN) ** -0.5, 0.625, ((0, 4),))
    filters_two = noise(arg_keys[2], (27 * C1 * C2,), (27 * C1) ** -0.5, 0.3125, ((0, 8),))
    cotangent = noise(arg_keys[3], (C2, NX, NY, CZ), 1.0, 6.0, ((1, 8), (2, 4)))
    return {"volume": volume, "filters_one": filters_one, "filters_two": filters_two, "cotangent": cotangent}


SLOPE = 0.3

def conv_valid(padded, kernel):
    result = lax.conv_general_dilated(padded[None], kernel, (1, 1, 1), 'VALID', dimension_numbers=('NCDHW', 'OIDHW', 'NCDHW'), preferred_element_type=jnp.float32)
    return result[0]

def kernel_grad(grad_out, padded):
    chans_out = grad_out.shape[0]
    chans_in = padded.shape[0]
    size_x, size_y, size_z = (grad_out.shape[1], grad_out.shape[2], grad_out.shape[3])
    flat_out = grad_out.reshape(chans_out, -1)
    pieces = []
    for shift_x in range(3):
        for shift_y in range(3):
            for shift_z in range(3):
                window = padded[:, shift_x:shift_x + size_x, shift_y:shift_y + size_y, shift_z:shift_z + size_z].reshape(chans_in, -1)
                pieces.append(lax.dot_general(flat_out, window, (((1,), (1,)), ((), ())), preferred_element_type=jnp.float32))
    return jnp.stack(pieces, axis=-1).reshape(-1)

def leaky(values):
    return jnp.where(values > 0, values, SLOPE * values)

def slope_of(values):
    return jnp.where(values > 0, jnp.float32(1.0), jnp.float32(SLOPE))

def pad_all(field):
    return jnp.pad(field, ((0, 0), (1, 1), (1, 1), (1, 1)))

def reference(volume, filters_one, filters_two, cotangent):
    kernel_one = filters_one.reshape(C1, CIN, 3, 3, 3)
    kernel_two = filters_two.reshape(C2, C1, 3, 3, 3)
    volume_pad = pad_all(volume)
    pre_one = conv_valid(volume_pad, kernel_one)
    hidden = leaky(pre_one).astype(jnp.bfloat16)
    hidden_pad = pad_all(hidden)
    pre_two = conv_valid(hidden_pad, kernel_two)
    activation = leaky(pre_two).astype(jnp.bfloat16)
    back_two = (cotangent.astype(jnp.float32) * slope_of(pre_two)).astype(jnp.bfloat16)
    flipped = jnp.flip(kernel_two, (2, 3, 4)).transpose(1, 0, 2, 3, 4)
    dhidden = conv_valid(pad_all(back_two), flipped)
    back_one = (dhidden * slope_of(pre_one)).astype(jnp.bfloat16)
    scale = 1.0 / math.sqrt(float(NX * NY * CZ))
    grad_two = kernel_grad(back_two, hidden_pad) * scale
    grad_one = kernel_grad(back_one, volume_pad) * scale
    return (activation, grad_one, grad_two)
```

```python
import functools
import math

import jax
import jax.numpy as jnp
from jax import lax
from jax.experimental import pallas as pl
from jax.experimental.pallas import tpu as pltpu
from jax.sharding import PartitionSpec as P

CIN = 4
C1 = 16
C2 = 32
SLOPE = 0.3
MESH = pl.DeviceIdType.MESH
F32 = jnp.float32
BF16 = jnp.bfloat16
DIRS = [(dx, dy) for dx in (-1, 0, 1) for dy in (-1, 0, 1) if (dx, dy) != (0, 0)]


def spans(delta, size, width):
    if delta == 1:
        return (size - width, width), (0, width)
    if delta == -1:
        return (0, width), (size + width, width)
    return (0, size), (width, size)


def leaky(values):
    return jnp.where(values > 0, values, SLOPE * values)


def exchange_kernel(
    n_space, n_samp, v_ref, c_ref, f1_ref, f2_ref, vp_ref, cp_ref, g1_ref, g2_ref,
    send_v, recv_v, send_c, recv_c, send_1, recv_1, send_2, recv_2,
):
    s = lax.axis_index("space")
    m = lax.axis_index("samp")
    size_x, size_y = v_ref.shape[0], v_ref.shape[1]

    vp_ref[...] = jnp.zeros_like(vp_ref)

    def zero_row(x, carry):
        cp_ref[x] = jnp.zeros(cp_ref.shape[1:], cp_ref.dtype)
        return carry

    lax.fori_loop(0, cp_ref.shape[0], zero_row, 0)

    def there(dx, dy):
        return (s + dx >= 0) & (s + dx < n_space) & (m + dy >= 0) & (m + dy < n_samp)

    barrier = pltpu.get_barrier_semaphore()
    peers = n_samp - 1 + n_space - 1
    for dx, dy in DIRS:
        if dx == 0 or dy == 0:
            continue
        peers = peers + jnp.where(there(dx, dy), 1, 0)

        @pl.when(there(dx, dy))
        def _():
            pl.semaphore_signal(barrier, inc=1, device_id=(s + dx, m + dy), device_id_type=MESH)
    for k in range(1, n_samp):
        pl.semaphore_signal(barrier, inc=1, device_id=(s, lax.rem(m + k, n_samp)), device_id_type=MESH)

    def greet(k, carry):
        pl.semaphore_signal(barrier, inc=1, device_id=(lax.rem(s + k, n_space), m), device_id_type=MESH)
        return carry

    lax.fori_loop(1, n_space, greet, 0)
    pl.semaphore_wait(barrier, peers)

    def copy_1(k):
        return pltpu.make_async_remote_copy(
            src_ref=f1_ref, dst_ref=g1_ref.at[m], send_sem=send_1.at[k], recv_sem=recv_1.at[k],
            device_id=(s, lax.rem(m + k, n_samp)), device_id_type=MESH)

    def copy_2(k):
        return pltpu.make_async_remote_copy(
            src_ref=f2_ref, dst_ref=g2_ref.at[s], send_sem=send_2.at[k], recv_sem=recv_2.at[k],
            device_id=(lax.rem(s + k, n_space), m), device_id_type=MESH)

    def halo(src, dst, width, send, recv, slot, dx, dy):
        (sx, nx), (tx, _) = spans(dx, size_x, width)
        (sy, ny), (ty, _) = spans(dy, size_y, width)
        return pltpu.make_async_remote_copy(
            src_ref=src.at[pl.ds(sx, nx), pl.ds(sy, ny)], dst_ref=dst.at[pl.ds(tx, nx), pl.ds(ty, ny)],
            send_sem=send.at[slot], recv_sem=recv.at[slot],
            device_id=(jnp.clip(s + dx, 0, n_space - 1), jnp.clip(m + dy, 0, n_samp - 1)),
            device_id_type=MESH)

    vol = [halo(v_ref, vp_ref, 3, send_v, recv_v, j, dx, dy) for j, (dx, dy) in enumerate(DIRS)]
    cot = [halo(c_ref, cp_ref, 1, send_c, recv_c, j, dx, dy) for j, (dx, dy) in enumerate(DIRS)]
    for k in range(1, n_samp):
        copy_1(k).start()

    def start_2(k, carry):
        copy_2(k).start()
        return carry

    lax.fori_loop(1, n_space, start_2, 0)
    for group in (vol, cot):
        for copy, (dx, dy) in zip(group, DIRS):
            @pl.when(there(dx, dy))
            def _():
                copy.start()

    g1_ref[m] = f1_ref[...]
    g2_ref[s] = f2_ref[...]
    vp_ref[3 : 3 + size_x, 3 : 3 + size_y] = v_ref[...]

    def centre(x, carry):
        cp_ref[x + 1, 1 : 1 + size_y] = c_ref[x]
        return carry

    lax.fori_loop(0, size_x, centre, 0)

    for k in range(1, n_samp):
        copy_1(k).wait()

    def wait_2(k, carry):
        copy_2(k).wait()
        return carry

    lax.fori_loop(1, n_space, wait_2, 0)
    for group in (vol, cot):
        for copy, (dx, dy) in zip(group, DIRS):
            @pl.when(there(-dx, -dy))
            def _():
                copy.wait_recv()

            @pl.when(there(dx, dy))
            def _():
                copy.wait_send()


def tap_sum(t, rows, lane, last):
    low = jnp.where(lane == 0, 0.0, pltpu.roll(t[:rows], 1, axis=1))
    high = jnp.where(lane == last, 0.0, pltpu.roll(t[2 * rows :], last, axis=1))
    return t[rows : 2 * rows] + low + high


def tap_spread(b, lane, last):
    low = jnp.where(lane == last, 0.0, pltpu.roll(b, last, axis=1))
    high = jnp.where(lane == 0, 0.0, pltpu.roll(b, 1, axis=1))
    return jnp.concatenate([low, b, high], axis=0)


def dot(a, b):
    return lax.dot_general(a, b, (((1,), (0,)), ((), ())), preferred_element_type=F32)


def dot_nt(a, b):
    return lax.dot_general(a, b, (((1,), (1,)), ((), ())), preferred_element_type=F32)


def compute_kernel(
    n_space, n_samp, v_ref, c_ref, w1_ref, w2_ref, w3_ref, act_ref, o1_ref, o2_ref,
    a1, a2, a3, hid, back, pre, t1, perm, acc1, acc2, act,
):
    s = lax.axis_index("space")
    m = lax.axis_index("samp")
    size_z = v_ref.shape[-1]
    last = size_z - 1
    size_x, size_y = act_ref.shape[1], act_ref.shape[2]
    high_y = size_y + 4

    def lanes(rows):
        return lax.broadcasted_iota(jnp.int32, (rows, size_z), 1)

    lane1 = lanes(C1)
    lane2 = lanes(C2)
    base1 = w1_ref[...]
    for y in range(high_y):
        row = base1 if y == 0 else pltpu.roll(base1, 4 * y, axis=1)
        a1[48 * y : 48 * y + 48] = row[:, :192].astype(BF16)
    base2 = w2_ref[...]
    a2[:96] = base2[:, :192].astype(BF16)
    a2[96:] = pltpu.roll(base2, 16, axis=1)[:, :192].astype(BF16)
    base3 = w3_ref[...]
    a3[:48] = base3.astype(BF16)
    a3[48:] = pltpu.roll(base3, 32, axis=1).astype(BF16)
    r = lax.broadcasted_iota(jnp.int32, (C2 * size_y, C2 * size_y), 0)
    q = lax.broadcasted_iota(jnp.int32, (C2 * size_y, C2 * size_y), 1)
    from_row = (r % size_y) * C2 + r // size_y
    perm[...] = jnp.where(q == from_row, 1.0, 0.0).astype(BF16)
    acc1[...] = jnp.zeros_like(acc1)
    acc2[...] = jnp.zeros_like(acc2)

    def vwin(x):
        return jnp.concatenate([v_ref[x], v_ref[x + 1], v_ref[x + 2]], axis=0)

    def layer1(x, carry):
        gx = s * size_x + x - 2
        ok_x = (gx >= 0) & (gx < n_space * size_x)
        t1[...] = dot(a1[...], vwin(x))
        for y in range(high_y):
            gy = m * size_y + y - 2
            ok = ok_x & (gy >= 0) & (gy < n_samp * size_y)
            p = tap_sum(t1[48 * y : 48 * y + 48], C1, lane1, last)
            pre[x, 16 * y : 16 * y + 16] = p
            h = leaky(p) * jnp.where(ok, 1.0, 0.0)
            hid[x, 16 * y : 16 * y + 16] = h.astype(BF16)
        return carry

    lax.fori_loop(0, size_x + 4, layer1, 0)

    def hwin(x, y):
        return jnp.concatenate([hid[x + k, 16 * y : 16 * y + 64] for k in range(3)], axis=0)

    def layer2(x, carry):
        for y in range(0, size_y + 2, 2):
            t = dot(a2[...], hwin(x, y))
            for half in range(2):
                p = tap_sum(t[96 * half : 96 * half + 96], C2, lane2, last)
                rows = slice(C2 * (y + half), C2 * (y + half) + C2)
                act[x, rows] = leaky(p).astype(BF16)
                b = c_ref[x, y + half].astype(F32) * jnp.where(p > 0, 1.0, SLOPE)
                back[x, rows] = b.astype(BF16)
        return carry

    lax.fori_loop(0, size_x + 2, layer2, 0)

    def finish(x, carry):
        value = dot(perm[...], act[x + 1, C2 : C2 + C2 * size_y])
        act_ref[:, x] = value.reshape(C2, size_y, size_z).astype(BF16)
        pieces = []
        for y in range(0, size_y, 2):
            win = jnp.concatenate([back[x + k, C2 * y : C2 * y + 128] for k in range(3)], axis=0)
            t = dot(a3[...], win)
            both = []
            for half in range(2):
                d = tap_sum(t[48 * half : 48 * half + 48], C1, lane1, last)
                p = pre[x + 2, 16 * (y + half + 2) : 16 * (y + half + 2) + 16]
                b1 = d * jnp.where(p > 0, 1.0, SLOPE)
                b1 = b1.astype(BF16).astype(F32)
                pieces.append(tap_spread(b1, lane1, last).astype(BF16))
                start = C2 * (y + half + 1)
                b2 = back[x + 1, start : start + C2].astype(F32)
                both.append(tap_spread(b2, lane2, last).astype(BF16))
            acc2[...] += dot_nt(jnp.concatenate(both, axis=0), hwin(x + 1, y + 1))
        acc1[...] += dot_nt(jnp.concatenate(pieces, axis=0), vwin(x + 2))
        return carry

    lax.fori_loop(0, size_x, finish, 0)

    def wide(values, rows):
        return jnp.concatenate([values, jnp.zeros((rows, 64), F32)], axis=1)

    o2_ref[...] = wide(acc2[:96], 96) + pltpu.roll(wide(acc2[96:], 96), 256 - 16, axis=1)
    total = jnp.zeros((48, 256), F32)
    for y in range(size_y):
        total = total + pltpu.roll(wide(acc1[48 * y : 48 * y + 48], 48), 256 - 4 * (y + 2), axis=1)
    o1_ref[...] = total


def reduce_kernel(
    n_space, n_samp, scale, g1_ref, g2_ref, o1_ref, o2_ref,
    part1, part2, full1, full2, mine1, mine2, send_a1, recv_a1, send_a2, recv_a2, send_b1, recv_b1, send_b2, recv_b2,
):
    s = lax.axis_index("space")
    m = lax.axis_index("samp")
    barrier = pltpu.get_barrier_semaphore()

    def samp_peer(k):
        return lax.rem(m + k, n_samp)

    def space_peer(k):
        return lax.rem(s + k, n_space)

    for k in range(1, n_samp):
        pl.semaphore_signal(barrier, inc=1, device_id=(s, samp_peer(k)), device_id_type=MESH)

    def over_space(body):
        def step(k, carry):
            body(k)
            return carry

        lax.fori_loop(1, n_space, step, 0)

    over_space(lambda k: pl.semaphore_signal(
        barrier, inc=1, device_id=(space_peer(k), m), device_id_type=MESH))
    pl.semaphore_wait(barrier, n_samp - 1 + n_space - 1)

    def first_1(k):
        return pltpu.make_async_remote_copy(
            src_ref=g1_ref.at[samp_peer(k)], dst_ref=part1.at[m], send_sem=send_a1.at[k],
            recv_sem=recv_a1.at[k], device_id=(s, samp_peer(k)), device_id_type=MESH)

    def first_2(k):
        return pltpu.make_async_remote_copy(
            src_ref=g2_ref.at[space_peer(k)], dst_ref=part2.at[s], send_sem=send_a2.at[k],
            recv_sem=recv_a2.at[k], device_id=(space_peer(k), m), device_id_type=MESH)

    def second_1(k):
        return pltpu.make_async_remote_copy(
            src_ref=mine1, dst_ref=full1.at[s], send_sem=send_b1.at[k],
            recv_sem=recv_b1.at[k], device_id=(space_peer(k), m), device_id_type=MESH)

    def second_2(k):
        return pltpu.make_async_remote_copy(
            src_ref=mine2, dst_ref=full2.at[m], send_sem=send_b2.at[k],
            recv_sem=recv_b2.at[k], device_id=(s, samp_peer(k)), device_id_type=MESH)

    over_space(lambda k: first_2(k).start())
    for k in range(1, n_samp):
        first_1(k).start()
    part1[m] = g1_ref[m]
    part2[s] = g2_ref[s]
    for k in range(1, n_samp):
        first_1(k).wait()
    mine1[...] = jnp.sum(part1[...], axis=0)
    over_space(lambda k: second_1(k).start())
    over_space(lambda k: first_2(k).wait())
    mine2[...] = jnp.sum(part2[...], axis=0)
    for k in range(1, n_samp):
        second_2(k).start()
    full1[s] = mine1[...]
    full2[m] = mine2[...]
    over_space(lambda k: second_1(k).wait())
    for k in range(1, n_samp):
        second_2(k).wait()
    o1_ref[...] = jnp.sum(full1[...], axis=0) * scale
    o2_ref[...] = jnp.sum(full2[...], axis=0) * scale


VMEM = pl.BlockSpec(memory_space=pltpu.VMEM)


def on_device(n_space, n_samp, volume, filters_one, filters_two, cotangent):
    _, size_x, size_y, size_z = volume.shape
    len1 = filters_one.shape[0]
    len2 = filters_two.shape[0]
    sem = pltpu.SemaphoreType.DMA
    v_rows = volume.transpose(1, 2, 0, 3)
    c_rows = cotangent.transpose(1, 2, 0, 3)
    vp, cp, all1, all2 = pl.pallas_call(
        functools.partial(exchange_kernel, n_space, n_samp),
        out_shape=[
            jax.ShapeDtypeStruct((size_x + 6, size_y + 8, CIN, size_z), BF16),
            jax.ShapeDtypeStruct((size_x + 2, size_y + 2, C2, size_z), BF16),
            jax.ShapeDtypeStruct((n_samp, 1, len1), BF16),
            jax.ShapeDtypeStruct((n_space, 1, len2), BF16),
        ],
        in_specs=[VMEM] * 4,
        out_specs=[VMEM] * 4,
        scratch_shapes=[
            sem((8,)), sem((8,)), sem((8,)), sem((8,)),
            sem((n_samp,)), sem((n_samp,)), sem((n_space,)), sem((n_space,)),
        ],
        compiler_params=pltpu.CompilerParams(
            collective_id=0, has_side_effects=True, vmem_limit_bytes=40 * 2**20),
    )(v_rows, c_rows, filters_one.reshape(1, len1), filters_two.reshape(1, len2))

    kern1 = all1.reshape(C1, CIN, 3, 3, 3).astype(F32)
    kern2 = all2.reshape(C2, C1, 3, 3, 3).astype(F32)
    base1 = kern1.transpose(4, 0, 2, 3, 1).reshape(3 * C1, 3, 3 * CIN)
    base1 = jnp.pad(base1, ((0, 0), (0, 0), (0, 64 - 3 * CIN))).reshape(3 * C1, 192)
    base1 = jnp.pad(base1, ((0, 0), (0, 64)))
    base2 = kern2.transpose(4, 0, 2, 3, 1).reshape(3 * C2, 3, 3 * C1)
    base2 = jnp.pad(base2, ((0, 0), (0, 0), (0, 64 - 3 * C1))).reshape(3 * C2, 192)
    base2 = jnp.pad(base2, ((0, 0), (0, 64)))
    base3 = jnp.flip(kern2, (2, 3, 4)).transpose(4, 1, 2, 3, 0).reshape(3 * C1, 3, 3 * C2)
    base3 = jnp.pad(base3, ((0, 0), (0, 0), (0, 128 - 3 * C2))).reshape(3 * C1, 384)

    high_y = size_y + 4
    activation, grad1, grad2 = pl.pallas_call(
        functools.partial(compute_kernel, n_space, n_samp),
        out_shape=[
            jax.ShapeDtypeStruct((C2, size_x, size_y, size_z), BF16),
            jax.ShapeDtypeStruct((48, 256), F32),
            jax.ShapeDtypeStruct((96, 256), F32),
        ],
        in_specs=[VMEM] * 5,
        out_specs=[VMEM] * 3,
        scratch_shapes=[
            pltpu.VMEM((48 * high_y, 192), BF16),
            pltpu.VMEM((192, 192), BF16),
            pltpu.VMEM((96, 384), BF16),
            pltpu.VMEM((size_x + 4, 16 * high_y, size_z), BF16),
            pltpu.VMEM((size_x + 2, C2 * (size_y + 2), size_z), BF16),
            pltpu.VMEM((size_x + 4, 16 * high_y, size_z), F32),
            pltpu.VMEM((48 * high_y, size_z), F32),
            pltpu.VMEM((C2 * size_y, C2 * size_y), BF16),
            pltpu.VMEM((48 * size_y, 192), F32),
            pltpu.VMEM((192, 192), F32),
            pltpu.VMEM((size_x + 2, C2 * (size_y + 2), size_z), BF16),
        ],
        compiler_params=pltpu.CompilerParams(vmem_limit_bytes=48 * 2**20),
    )(vp.reshape(size_x + 6, CIN * (size_y + 8), size_z), cp, base1, base2, base3)

    grad1 = grad1[:, :192].reshape(3, C1, 3, 64)[..., : 3 * CIN].reshape(3, C1, 3, 3, CIN)
    grad1 = grad1.transpose(1, 4, 2, 3, 0).reshape(n_samp, 1, len1)
    grad2 = grad2[:, :192].reshape(3, C2, 3, 64)[..., : 3 * C1].reshape(3, C2, 3, 3, C1)
    grad2 = grad2.transpose(1, 4, 2, 3, 0).reshape(n_space, 1, len2)
    scale = 1.0 / math.sqrt(float(size_x * n_space * size_y * n_samp * size_z))
    out1, out2 = pl.pallas_call(
        functools.partial(reduce_kernel, n_space, n_samp, scale),
        out_shape=[
            jax.ShapeDtypeStruct((1, len1), F32),
            jax.ShapeDtypeStruct((1, len2), F32),
        ],
        in_specs=[VMEM] * 2,
        out_specs=[VMEM] * 2,
        scratch_shapes=[
            pltpu.VMEM((n_samp, 1, len1), F32),
            pltpu.VMEM((n_space, 1, len2), F32),
            pltpu.VMEM((n_space, 1, len1), F32),
            pltpu.VMEM((n_samp, 1, len2), F32),
            pltpu.VMEM((1, len1), F32),
            pltpu.VMEM((1, len2), F32),
            sem((n_samp,)), sem((n_samp,)), sem((n_space,)), sem((n_space,)),
            sem((n_space,)), sem((n_space,)), sem((n_samp,)), sem((n_samp,)),
        ],
        compiler_params=pltpu.CompilerParams(collective_id=1, has_side_effects=True),
    )(grad1, grad2)
    return activation, out1.reshape(len1), out2.reshape(len2)


def solution(mesh):
    in_specs = (
        P(None, "space", "samp", None),
        P("samp"),
        P("space"),
        P(None, "space", "samp", None),
    )
    out_specs = (P(None, "space", "samp", None), P("samp"), P("space"))
    return jax.shard_map(
        functools.partial(on_device, mesh.shape["space"], mesh.shape["samp"]),
        mesh=mesh, in_specs=in_specs, out_specs=out_specs, check_vma=False,
    )
```

```python
import functools
import math

import jax
import jax.numpy as jnp
from jax import lax
from jax.experimental import pallas as pl
from jax.experimental.pallas import tpu as pltpu
from jax.sharding import PartitionSpec as P

CIN = 4
C1 = 16
C2 = 32
SLOPE = 0.3
MESH = pl.DeviceIdType.MESH
F32 = jnp.float32
BF16 = jnp.bfloat16
DIRS = [(dx, dy) for dx in (-1, 0, 1) for dy in (-1, 0, 1) if (dx, dy) != (0, 0)]


def spans(delta, size, width):
    if delta == 1:
        return (size - width, width), (0, width)
    if delta == -1:
        return (0, width), (size + width, width)
    return (0, size), (width, size)


def leaky(values):
    return jnp.where(values > 0, values, SLOPE * values)


def exchange_kernel(
    n_space, n_samp, v_ref, c_ref, f1_ref, f2_ref, vp_ref, cp_ref, g1_ref, g2_ref,
    send_v, recv_v, send_c, recv_c, send_1, recv_1, send_2, recv_2,
):
    s = lax.axis_index("space")
    m = lax.axis_index("samp")
    size_x, size_y = v_ref.shape[0], v_ref.shape[1]

    vp_ref[...] = jnp.zeros_like(vp_ref)

    def zero_row(x, carry):
        cp_ref[x] = jnp.zeros(cp_ref.shape[1:], cp_ref.dtype)
        return carry

    lax.fori_loop(0, cp_ref.shape[0], zero_row, 0)

    def there(dx, dy):
        return (s + dx >= 0) & (s + dx < n_space) & (m + dy >= 0) & (m + dy < n_samp)

    barrier = pltpu.get_barrier_semaphore()
    peers = n_samp - 1 + n_space - 1
    for dx, dy in DIRS:
        if dx == 0 or dy == 0:
            continue
        peers = peers + jnp.where(there(dx, dy), 1, 0)

        @pl.when(there(dx, dy))
        def _():
            pl.semaphore_signal(barrier, inc=1, device_id=(s + dx, m + dy), device_id_type=MESH)
    for k in range(1, n_samp):
        pl.semaphore_signal(barrier, inc=1, device_id=(s, lax.rem(m + k, n_samp)), device_id_type=MESH)

    def greet(k, carry):
        pl.semaphore_signal(barrier, inc=1, device_id=(lax.rem(s + k, n_space), m), device_id_type=MESH)
        return carry

    lax.fori_loop(1, n_space, greet, 0)
    pl.semaphore_wait(barrier, peers)

    def copy_1(k):
        return pltpu.make_async_remote_copy(
            src_ref=f1_ref, dst_ref=g1_ref.at[m], send_sem=send_1.at[k], recv_sem=recv_1.at[k],
            device_id=(s, lax.rem(m + k, n_samp)), device_id_type=MESH)

    def copy_2(k):
        return pltpu.make_async_remote_copy(
            src_ref=f2_ref, dst_ref=g2_ref.at[s], send_sem=send_2.at[k], recv_sem=recv_2.at[k],
            device_id=(lax.rem(s + k, n_space), m), device_id_type=MESH)

    def halo(src, dst, width, send, recv, slot, dx, dy):
        (sx, nx), (tx, _) = spans(dx, size_x, width)
        (sy, ny), (ty, _) = spans(dy, size_y, width)
        return pltpu.make_async_remote_copy(
            src_ref=src.at[pl.ds(sx, nx), pl.ds(sy, ny)], dst_ref=dst.at[pl.ds(tx, nx), pl.ds(ty, ny)],
            send_sem=send.at[slot], recv_sem=recv.at[slot],
            device_id=(jnp.clip(s + dx, 0, n_space - 1), jnp.clip(m + dy, 0, n_samp - 1)),
            device_id_type=MESH)

    vol = [halo(v_ref, vp_ref, 3, send_v, recv_v, j, dx, dy) for j, (dx, dy) in enumerate(DIRS)]
    cot = [halo(c_ref, cp_ref, 1, send_c, recv_c, j, dx, dy) for j, (dx, dy) in enumerate(DIRS)]
    for k in range(1, n_samp):
        copy_1(k).start()

    def start_2(k, carry):
        copy_2(k).start()
        return carry

    lax.fori_loop(1, n_space, start_2, 0)
    for group in (vol, cot):
        for copy, (dx, dy) in zip(group, DIRS):
            @pl.when(there(dx, dy))
            def _():
                copy.start()

    g1_ref[m] = f1_ref[...]
    g2_ref[s] = f2_ref[...]
    vp_ref[3 : 3 + size_x, 3 : 3 + size_y] = v_ref[...]

    def centre(x, carry):
        cp_ref[x + 1, 1 : 1 + size_y] = c_ref[x]
        return carry

    lax.fori_loop(0, size_x, centre, 0)

    for k in range(1, n_samp):
        copy_1(k).wait()

    def wait_2(k, carry):
        copy_2(k).wait()
        return carry

    lax.fori_loop(1, n_space, wait_2, 0)
    for group in (vol, cot):
        for copy, (dx, dy) in zip(group, DIRS):
            @pl.when(there(-dx, -dy))
            def _():
                copy.wait_recv()

            @pl.when(there(dx, dy))
            def _():
                copy.wait_send()


def tap_sum(t, rows, lane, last):
    low = jnp.where(lane == 0, 0.0, pltpu.roll(t[:rows], 1, axis=1))
    high = jnp.where(lane == last, 0.0, pltpu.roll(t[2 * rows :], last, axis=1))
    return t[rows : 2 * rows] + low + high


def tap_spread(b, lane, last):
    low = jnp.where(lane == last, 0.0, pltpu.roll(b, last, axis=1))
    high = jnp.where(lane == 0, 0.0, pltpu.roll(b, 1, axis=1))
    return jnp.concatenate([low, b, high], axis=0)


def dot(a, b):
    return lax.dot_general(a, b, (((1,), (0,)), ((), ())), preferred_element_type=F32)


def dot_nt(a, b):
    return lax.dot_general(a, b, (((1,), (1,)), ((), ())), preferred_element_type=F32)


def one_hot(rows, source):
    row = lax.broadcasted_iota(jnp.int32, (rows, source.shape[1]), 0)
    return jnp.where(row == source, 1.0, 0.0).astype(BF16)


def build_selectors(q1, q2, q3):
    lane = lax.broadcasted_iota(jnp.int32, (1, 256), 1)
    kx, ky, i = lane >> 6, (lane >> 2) & 15, lane & 3
    source1 = jnp.where((kx < 3) & (ky < 3), i * 27 + kx * 9 + ky * 3, -9)
    kx, ky, i = lane >> 6, (lane >> 4) & 3, lane & 15
    source2 = jnp.where((kx < 3) & (ky < 3), i * 27 + kx * 9 + ky * 3, -9)
    for kz in range(3):
        q1[kz] = one_hot(27 * CIN, source1 + kz)
        q2[kz] = one_hot(27 * C1, source2 + kz)
    lane = lax.broadcasted_iota(jnp.int32, (1, 128), 1)
    kz, i = lane >> 4, lane & 15
    for kx in range(3):
        for ky in range(3):
            source3 = jnp.where(kz < 3, i * 27 + (2 - kx) * 9 + (2 - ky) * 3 + 2 - kz, -9)
            q3[3 * kx + ky] = one_hot(27 * C1, source3)


def gather_rows(all_ref, rows_ref, wide_ref):
    owners, count, unit = all_ref.shape
    for j in range(owners):
        rows_ref[count * j : count * (j + 1)] = all_ref[j].astype(F32)
    split = wide_ref.shape[1] // unit
    if split == 1:
        return rows_ref[...].astype(BF16)
    for k in range(split):
        wide_ref[:, unit * k : unit * (k + 1)] = rows_ref[pl.ds(k, wide_ref.shape[0], stride=split)]
    return wide_ref[...].astype(BF16)


def scatter_rows(value, rows_ref, wide_ref, out_ref):
    owners, count, unit = out_ref.shape
    split = value.shape[1] // unit
    if split == 1:
        rows_ref[...] = value
    else:
        wide_ref[...] = value
        for k in range(split):
            rows_ref[pl.ds(k, value.shape[0], stride=split)] = wide_ref[:, unit * k : unit * (k + 1)]
    for j in range(owners):
        out_ref[j] = rows_ref[count * j : count * (j + 1)]


def flat_order(grad, q, chans):
    result = 0.0
    for kz in range(3):
        g = grad[chans * kz : chans * (kz + 1)]
        high = g.astype(BF16)
        rest = g - high.astype(F32)
        mid = rest.astype(BF16)
        low = (rest - mid.astype(F32)).astype(BF16)
        r = dot_nt(jnp.concatenate([high, mid, low], axis=0), q[kz])
        result = result + (r[:chans] + r[chans : 2 * chans] + r[2 * chans :])
    return result


def compute_kernel(
    n_space, n_samp, vp_ref, c_ref, all1_ref, all2_ref, act_ref, o1_ref, o2_ref,
    a1, a2, a3, hid, back, pre, t1, perm, acc1, acc2, act,
    q1, q2, q3, rows1, wide1, rows2, wide2, tall3, vf, v_ref,
):
    s = lax.axis_index("space")
    m = lax.axis_index("samp")
    size_z = vp_ref.shape[-1]
    last = size_z - 1
    build_selectors(q1, q2, q3)
    m1 = gather_rows(all1_ref, rows1, wide1)
    m2 = gather_rows(all2_ref, rows2, wide2)
    base1 = jnp.concatenate([dot(m1, q1[kz]) for kz in range(3)], axis=0)
    base2 = jnp.concatenate([dot(m2, q2[kz]) for kz in range(3)], axis=0)
    tall3[...] = jnp.zeros_like(tall3)
    for kx in range(3):
        for ky in range(3):
            start = 128 * kx + C2 * ky
            tall3[start : start + C2] = dot(m2, q3[3 * kx + ky])
    base3 = tall3[...].T[:48]

    def lift(x, carry):
        for y in range(vp_ref.shape[1]):
            vf[CIN * y : CIN * (y + 1)] = vp_ref[x, y].astype(F32)
        v_ref[x] = vf[...].astype(BF16)
        return carry

    lax.fori_loop(0, vp_ref.shape[0], lift, 0)
    size_x, size_y = act_ref.shape[1], act_ref.shape[2]
    high_y = size_y + 4

    def lanes(rows):
        return lax.broadcasted_iota(jnp.int32, (rows, size_z), 1)

    lane1 = lanes(C1)
    lane2 = lanes(C2)
    for y in range(high_y):
        row = base1 if y == 0 else pltpu.roll(base1, 4 * y, axis=1)
        a1[48 * y : 48 * y + 48] = row[:, :192].astype(BF16)
    a2[:96] = base2[:, :192].astype(BF16)
    a2[96:] = pltpu.roll(base2, 16, axis=1)[:, :192].astype(BF16)
    a3[:48] = base3.astype(BF16)
    a3[48:] = pltpu.roll(base3, 32, axis=1).astype(BF16)
    r = lax.broadcasted_iota(jnp.int32, (C2 * size_y, C2 * size_y), 0)
    q = lax.broadcasted_iota(jnp.int32, (C2 * size_y, C2 * size_y), 1)
    from_row = (r % size_y) * C2 + r // size_y
    perm[...] = jnp.where(q == from_row, 1.0, 0.0).astype(BF16)
    acc1[...] = jnp.zeros_like(acc1)
    acc2[...] = jnp.zeros_like(acc2)

    def vwin(x):
        return jnp.concatenate([v_ref[x], v_ref[x + 1], v_ref[x + 2]], axis=0)

    def layer1(x, carry):
        gx = s * size_x + x - 2
        ok_x = (gx >= 0) & (gx < n_space * size_x)
        t1[...] = dot(a1[...], vwin(x))
        for y in range(high_y):
            gy = m * size_y + y - 2
            ok = ok_x & (gy >= 0) & (gy < n_samp * size_y)
            p = tap_sum(t1[48 * y : 48 * y + 48], C1, lane1, last)
            pre[x, 16 * y : 16 * y + 16] = p
            h = leaky(p) * jnp.where(ok, 1.0, 0.0)
            hid[x, 16 * y : 16 * y + 16] = h.astype(BF16)
        return carry

    lax.fori_loop(0, size_x + 4, layer1, 0)

    def hwin(x, y):
        return jnp.concatenate([hid[x + k, 16 * y : 16 * y + 64] for k in range(3)], axis=0)

    def layer2(x, carry):
        for y in range(0, size_y + 2, 2):
            t = dot(a2[...], hwin(x, y))
            for half in range(2):
                p = tap_sum(t[96 * half : 96 * half + 96], C2, lane2, last)
                rows = slice(C2 * (y + half), C2 * (y + half) + C2)
                act[x, rows] = leaky(p).astype(BF16)
                b = c_ref[x, y + half].astype(F32) * jnp.where(p > 0, 1.0, SLOPE)
                back[x, rows] = b.astype(BF16)
        return carry

    lax.fori_loop(0, size_x + 2, layer2, 0)

    def finish(x, carry):
        value = dot(perm[...], act[x + 1, C2 : C2 + C2 * size_y])
        act_ref[:, x] = value.reshape(C2, size_y, size_z).astype(BF16)
        pieces = []
        for y in range(0, size_y, 2):
            win = jnp.concatenate([back[x + k, C2 * y : C2 * y + 128] for k in range(3)], axis=0)
            t = dot(a3[...], win)
            both = []
            for half in range(2):
                d = tap_sum(t[48 * half : 48 * half + 48], C1, lane1, last)
                p = pre[x + 2, 16 * (y + half + 2) : 16 * (y + half + 2) + 16]
                b1 = d * jnp.where(p > 0, 1.0, SLOPE)
                b1 = b1.astype(BF16).astype(F32)
                pieces.append(tap_spread(b1, lane1, last).astype(BF16))
                start = C2 * (y + half + 1)
                b2 = back[x + 1, start : start + C2].astype(F32)
                both.append(tap_spread(b2, lane2, last).astype(BF16))
            acc2[...] += dot_nt(jnp.concatenate(both, axis=0), hwin(x + 1, y + 1))
        acc1[...] += dot_nt(jnp.concatenate(pieces, axis=0), vwin(x + 2))
        return carry

    lax.fori_loop(0, size_x, finish, 0)

    def wide(values, rows):
        return jnp.concatenate([values, jnp.zeros((rows, 64), F32)], axis=1)

    total2 = wide(acc2[:96], 96) + pltpu.roll(wide(acc2[96:], 96), 256 - 16, axis=1)
    total = jnp.zeros((48, 256), F32)
    for y in range(size_y):
        total = total + pltpu.roll(wide(acc1[48 * y : 48 * y + 48], 48), 256 - 4 * (y + 2), axis=1)
    scatter_rows(flat_order(total, q1, C1), rows1, wide1, o1_ref)
    scatter_rows(flat_order(total2, q2, C2), rows2, wide2, o2_ref)


def reduce_kernel(
    n_space, n_samp, scale, g1_ref, g2_ref, o1_ref, o2_ref,
    part1, part2, full1, full2, mine1, mine2, send_a1, recv_a1, send_a2, recv_a2, send_b1, recv_b1, send_b2, recv_b2,
):
    s = lax.axis_index("space")
    m = lax.axis_index("samp")
    barrier = pltpu.get_barrier_semaphore()

    def samp_peer(k):
        return lax.rem(m + k, n_samp)

    def space_peer(k):
        return lax.rem(s + k, n_space)

    for k in range(1, n_samp):
        pl.semaphore_signal(barrier, inc=1, device_id=(s, samp_peer(k)), device_id_type=MESH)

    def over_space(body):
        def step(k, carry):
            body(k)
            return carry

        lax.fori_loop(1, n_space, step, 0)

    over_space(lambda k: pl.semaphore_signal(
        barrier, inc=1, device_id=(space_peer(k), m), device_id_type=MESH))
    pl.semaphore_wait(barrier, n_samp - 1 + n_space - 1)

    def first_1(k):
        return pltpu.make_async_remote_copy(
            src_ref=g1_ref.at[samp_peer(k)], dst_ref=part1.at[m], send_sem=send_a1.at[k],
            recv_sem=recv_a1.at[k], device_id=(s, samp_peer(k)), device_id_type=MESH)

    def first_2(k):
        return pltpu.make_async_remote_copy(
            src_ref=g2_ref.at[space_peer(k)], dst_ref=part2.at[s], send_sem=send_a2.at[k],
            recv_sem=recv_a2.at[k], device_id=(space_peer(k), m), device_id_type=MESH)

    def second_1(k):
        return pltpu.make_async_remote_copy(
            src_ref=mine1, dst_ref=full1.at[s], send_sem=send_b1.at[k],
            recv_sem=recv_b1.at[k], device_id=(space_peer(k), m), device_id_type=MESH)

    def second_2(k):
        return pltpu.make_async_remote_copy(
            src_ref=mine2, dst_ref=full2.at[m], send_sem=send_b2.at[k],
            recv_sem=recv_b2.at[k], device_id=(s, samp_peer(k)), device_id_type=MESH)

    over_space(lambda k: first_2(k).start())
    for k in range(1, n_samp):
        first_1(k).start()
    part1[m] = g1_ref[m]
    part2[s] = g2_ref[s]
    for k in range(1, n_samp):
        first_1(k).wait()
    mine1[...] = jnp.sum(part1[...], axis=0)
    over_space(lambda k: second_1(k).start())
    over_space(lambda k: first_2(k).wait())
    mine2[...] = jnp.sum(part2[...], axis=0)
    for k in range(1, n_samp):
        second_2(k).start()
    full1[s] = mine1[...]
    full2[m] = mine2[...]
    over_space(lambda k: second_1(k).wait())
    for k in range(1, n_samp):
        second_2(k).wait()
    o1_ref[...] = jnp.sum(full1[...], axis=0) * scale
    o2_ref[...] = jnp.sum(full2[...], axis=0) * scale


VMEM = pl.BlockSpec(memory_space=pltpu.VMEM)


def on_device(n_space, n_samp, volume, filters_one, filters_two, cotangent):
    _, size_x, size_y, size_z = volume.shape
    len1 = filters_one.shape[0]
    len2 = filters_two.shape[0]
    unit1 = math.gcd(len1, 27 * CIN)
    unit2 = math.gcd(len2, 27 * C1)
    piece1 = (len1 // unit1, unit1)
    piece2 = (len2 // unit2, unit2)
    sem = pltpu.SemaphoreType.DMA
    v_rows = volume.transpose(1, 2, 0, 3)
    c_rows = cotangent.transpose(1, 2, 0, 3)
    vp, cp, all1, all2 = pl.pallas_call(
        functools.partial(exchange_kernel, n_space, n_samp),
        out_shape=[
            jax.ShapeDtypeStruct((size_x + 6, size_y + 8, CIN, size_z), BF16),
            jax.ShapeDtypeStruct((size_x + 2, size_y + 2, C2, size_z), BF16),
            jax.ShapeDtypeStruct((n_samp, *piece1), BF16),
            jax.ShapeDtypeStruct((n_space, *piece2), BF16),
        ],
        in_specs=[VMEM] * 4,
        out_specs=[VMEM] * 4,
        scratch_shapes=[
            sem((8,)), sem((8,)), sem((8,)), sem((8,)),
            sem((n_samp,)), sem((n_samp,)), sem((n_space,)), sem((n_space,)),
        ],
        compiler_params=pltpu.CompilerParams(
            collective_id=0, has_side_effects=True, vmem_limit_bytes=40 * 2**20),
    )(v_rows, c_rows, filters_one.reshape(piece1), filters_two.reshape(piece2))

    high_y = size_y + 4
    activation, grad1, grad2 = pl.pallas_call(
        functools.partial(compute_kernel, n_space, n_samp),
        out_shape=[
            jax.ShapeDtypeStruct((C2, size_x, size_y, size_z), BF16),
            jax.ShapeDtypeStruct((n_samp, *piece1), F32),
            jax.ShapeDtypeStruct((n_space, *piece2), F32),
        ],
        in_specs=[VMEM] * 4,
        out_specs=[VMEM] * 3,
        scratch_shapes=[
            pltpu.VMEM((48 * high_y, 192), BF16),
            pltpu.VMEM((192, 192), BF16),
            pltpu.VMEM((96, 384), BF16),
            pltpu.VMEM((size_x + 4, 16 * high_y, size_z), BF16),
            pltpu.VMEM((size_x + 2, C2 * (size_y + 2), size_z), BF16),
            pltpu.VMEM((size_x + 4, 16 * high_y, size_z), F32),
            pltpu.VMEM((48 * high_y, size_z), F32),
            pltpu.VMEM((C2 * size_y, C2 * size_y), BF16),
            pltpu.VMEM((48 * size_y, 192), F32),
            pltpu.VMEM((192, 192), F32),
            pltpu.VMEM((size_x + 2, C2 * (size_y + 2), size_z), BF16),
            pltpu.VMEM((3, 27 * CIN, 256), BF16),
            pltpu.VMEM((3, 27 * C1, 256), BF16),
            pltpu.VMEM((9, 27 * C1, 128), BF16),
            pltpu.VMEM((n_samp * piece1[0], piece1[1]), F32),
            pltpu.VMEM((C1, 27 * CIN), F32),
            pltpu.VMEM((n_space * piece2[0], piece2[1]), F32),
            pltpu.VMEM((C2, 27 * C1), F32),
            pltpu.VMEM((384, 128), F32),
            pltpu.VMEM((CIN * (size_y + 8), size_z), F32),
            pltpu.VMEM((size_x + 6, CIN * (size_y + 8), size_z), BF16),
        ],
        compiler_params=pltpu.CompilerParams(vmem_limit_bytes=48 * 2**20),
    )(vp, cp, all1, all2)

    scale = 1.0 / math.sqrt(float(size_x * n_space * size_y * n_samp * size_z))
    out1, out2 = pl.pallas_call(
        functools.partial(reduce_kernel, n_space, n_samp, scale),
        out_shape=[
            jax.ShapeDtypeStruct(piece1, F32),
            jax.ShapeDtypeStruct(piece2, F32),
        ],
        in_specs=[VMEM] * 2,
        out_specs=[VMEM] * 2,
        scratch_shapes=[
            pltpu.VMEM((n_samp, *piece1), F32),
            pltpu.VMEM((n_space, *piece2), F32),
            pltpu.VMEM((n_space, *piece1), F32),
            pltpu.VMEM((n_samp, *piece2), F32),
            pltpu.VMEM(piece1, F32),
            pltpu.VMEM(piece2, F32),
            sem((n_samp,)), sem((n_samp,)), sem((n_space,)), sem((n_space,)),
            sem((n_space,)), sem((n_space,)), sem((n_samp,)), sem((n_samp,)),
        ],
        compiler_params=pltpu.CompilerParams(collective_id=1, has_side_effects=True),
    )(grad1, grad2)
    return activation, out1.reshape(len1), out2.reshape(len2)


def solution(mesh):
    in_specs = (
        P(None, "space", "samp", None),
        P("samp"),
        P("space"),
        P(None, "space", "samp", None),
    )
    out_specs = (P(None, "space", "samp", None), P("samp"), P("space"))
    return jax.shard_map(
        functools.partial(on_device, mesh.shape["space"], mesh.shape["samp"]),
        mesh=mesh, in_specs=in_specs, out_specs=out_specs, check_vma=False,
    )
```

```python
import functools
import math

import jax
import jax.numpy as jnp
from jax import lax
from jax.experimental import pallas as pl
from jax.experimental.pallas import tpu as pltpu
from jax.sharding import PartitionSpec as P

CIN = 4
C1 = 16
C2 = 32
SLOPE = 0.3
MESH = pl.DeviceIdType.MESH
F32 = jnp.float32
BF16 = jnp.bfloat16
DIRS = [(dx, dy) for dx in (-1, 0, 1) for dy in (-1, 0, 1) if (dx, dy) != (0, 0)]


def spans(delta, size, width):
    if delta == 1:
        return (size - width, width), (0, width)
    if delta == -1:
        return (0, width), (size + width, width)
    return (0, size), (width, size)


def leaky(values):
    return jnp.where(values > 0, values, SLOPE * values)


def tap_sum(t, rows, lane, last):
    low = jnp.where(lane == 0, 0.0, pltpu.roll(t[:rows], 1, axis=1))
    high = jnp.where(lane == last, 0.0, pltpu.roll(t[2 * rows :], last, axis=1))
    return t[rows : 2 * rows] + low + high


def tap_spread(b, lane, last):
    low = jnp.where(lane == last, 0.0, pltpu.roll(b, last, axis=1))
    high = jnp.where(lane == 0, 0.0, pltpu.roll(b, 1, axis=1))
    return jnp.concatenate([low, b, high], axis=0)


def dot(a, b):
    return lax.dot_general(a, b, (((1,), (0,)), ((), ())), preferred_element_type=F32)


def dot_nt(a, b):
    return lax.dot_general(a, b, (((1,), (1,)), ((), ())), preferred_element_type=F32)


def one_hot(rows, source):
    row = lax.broadcasted_iota(jnp.int32, (rows, source.shape[1]), 0)
    return jnp.where(row == source, 1.0, 0.0).astype(BF16)


def build_selectors(q1, q2, q3):
    lane = lax.broadcasted_iota(jnp.int32, (1, 256), 1)
    kx, ky, i = lane >> 6, (lane >> 2) & 15, lane & 3
    source1 = jnp.where((kx < 3) & (ky < 3), i * 27 + kx * 9 + ky * 3, -9)
    kx, ky, i = lane >> 6, (lane >> 4) & 3, lane & 15
    source2 = jnp.where((kx < 3) & (ky < 3), i * 27 + kx * 9 + ky * 3, -9)
    for kz in range(3):
        q1[kz] = one_hot(27 * CIN, source1 + kz)
        q2[kz] = one_hot(27 * C1, source2 + kz)
    lane = lax.broadcasted_iota(jnp.int32, (1, 128), 1)
    kz, i = lane >> 4, lane & 15
    for kx in range(3):
        for ky in range(3):
            source3 = jnp.where(kz < 3, i * 27 + (2 - kx) * 9 + (2 - ky) * 3 + 2 - kz, -9)
            q3[3 * kx + ky] = one_hot(27 * C1, source3)


def gather_rows(all_ref, rows_ref, wide_ref):
    owners, count, unit = all_ref.shape
    for j in range(owners):
        rows_ref[count * j : count * (j + 1)] = all_ref[j].astype(F32)
    split = wide_ref.shape[1] // unit
    if split == 1:
        return rows_ref[...].astype(BF16)
    for k in range(split):
        wide_ref[:, unit * k : unit * (k + 1)] = rows_ref[pl.ds(k, wide_ref.shape[0], stride=split)]
    return wide_ref[...].astype(BF16)


def scatter_rows(value, rows_ref, wide_ref, out_ref):
    owners, count, unit = out_ref.shape
    split = value.shape[1] // unit
    if split == 1:
        rows_ref[...] = value
    else:
        wide_ref[...] = value
        for k in range(split):
            rows_ref[pl.ds(k, value.shape[0], stride=split)] = wide_ref[:, unit * k : unit * (k + 1)]
    for j in range(owners):
        out_ref[j] = rows_ref[count * j : count * (j + 1)]


def flat_order(grad, q, chans):
    result = 0.0
    for kz in range(3):
        g = grad[chans * kz : chans * (kz + 1)]
        high = g.astype(BF16)
        rest = g - high.astype(F32)
        mid = rest.astype(BF16)
        low = (rest - mid.astype(F32)).astype(BF16)
        r = dot_nt(jnp.concatenate([high, mid, low], axis=0), q[kz])
        result = result + (r[:chans] + r[chans : 2 * chans] + r[2 * chans :])
    return result


def fused_kernel(
    n_space, n_samp, scale, v_ref, c_ref, f1_ref, f2_ref, act_ref, o1_ref, o2_ref,
    vp, cp, all1, all2,
    a1, a2, a3, hid, back, pre, t1, perm, acc1, acc2, act,
    q1, q2, q3, rows1, wide1, rows2, wide2, tall3, vf, vrows,
    grad1, grad2, part1, part2, full1, full2, mine1, mine2,
    send_v, recv_v, send_c, recv_c, send_1, recv_1, send_2, recv_2,
    send_a1, recv_a1, send_a2, recv_a2, send_b1, recv_b1, send_b2, recv_b2,
):
    s = lax.axis_index("space")
    m = lax.axis_index("samp")
    size_x, size_y = v_ref.shape[0], v_ref.shape[1]

    vp[...] = jnp.zeros_like(vp)

    def zero_row(x, carry):
        cp[x] = jnp.zeros(cp.shape[1:], cp.dtype)
        return carry

    lax.fori_loop(0, cp.shape[0], zero_row, 0)

    def there(dx, dy):
        return (s + dx >= 0) & (s + dx < n_space) & (m + dy >= 0) & (m + dy < n_samp)

    barrier = pltpu.get_barrier_semaphore()
    peers = n_samp - 1 + n_space - 1
    for dx, dy in DIRS:
        if dx == 0 or dy == 0:
            continue
        peers = peers + jnp.where(there(dx, dy), 1, 0)

        @pl.when(there(dx, dy))
        def _():
            pl.semaphore_signal(barrier, inc=1, device_id=(s + dx, m + dy), device_id_type=MESH)
    for k in range(1, n_samp):
        pl.semaphore_signal(barrier, inc=1, device_id=(s, lax.rem(m + k, n_samp)), device_id_type=MESH)

    def greet(k, carry):
        pl.semaphore_signal(barrier, inc=1, device_id=(lax.rem(s + k, n_space), m), device_id_type=MESH)
        return carry

    lax.fori_loop(1, n_space, greet, 0)
    pl.semaphore_wait(barrier, peers)

    def copy_1(k):
        return pltpu.make_async_remote_copy(
            src_ref=f1_ref, dst_ref=all1.at[m], send_sem=send_1.at[k], recv_sem=recv_1.at[k],
            device_id=(s, lax.rem(m + k, n_samp)), device_id_type=MESH)

    def copy_2(k):
        return pltpu.make_async_remote_copy(
            src_ref=f2_ref, dst_ref=all2.at[s], send_sem=send_2.at[k], recv_sem=recv_2.at[k],
            device_id=(lax.rem(s + k, n_space), m), device_id_type=MESH)

    def halo(src, dst, width, send, recv, slot, dx, dy):
        (sx, nx), (tx, _) = spans(dx, size_x, width)
        (sy, ny), (ty, _) = spans(dy, size_y, width)
        return pltpu.make_async_remote_copy(
            src_ref=src.at[pl.ds(sx, nx), pl.ds(sy, ny)], dst_ref=dst.at[pl.ds(tx, nx), pl.ds(ty, ny)],
            send_sem=send.at[slot], recv_sem=recv.at[slot],
            device_id=(jnp.clip(s + dx, 0, n_space - 1), jnp.clip(m + dy, 0, n_samp - 1)),
            device_id_type=MESH)

    vol = [halo(v_ref, vp, 3, send_v, recv_v, j, dx, dy) for j, (dx, dy) in enumerate(DIRS)]
    cot = [halo(c_ref, cp, 1, send_c, recv_c, j, dx, dy) for j, (dx, dy) in enumerate(DIRS)]
    for k in range(1, n_samp):
        copy_1(k).start()

    def start_2(k, carry):
        copy_2(k).start()
        return carry

    lax.fori_loop(1, n_space, start_2, 0)
    for group in (vol, cot):
        for copy, (dx, dy) in zip(group, DIRS):
            @pl.when(there(dx, dy))
            def _():
                copy.start()

    all1[m] = f1_ref[...]
    all2[s] = f2_ref[...]
    vp[3 : 3 + size_x, 3 : 3 + size_y] = v_ref[...]

    def centre(x, carry):
        cp[x + 1, 1 : 1 + size_y] = c_ref[x]
        return carry

    lax.fori_loop(0, size_x, centre, 0)


    size_z = v_ref.shape[-1]
    last = size_z - 1
    high_y = size_y + 4

    def lanes(rows):
        return lax.broadcasted_iota(jnp.int32, (rows, size_z), 1)

    lane1 = lanes(C1)
    lane2 = lanes(C2)
    build_selectors(q1, q2, q3)
    r = lax.broadcasted_iota(jnp.int32, (C2 * size_y, C2 * size_y), 0)
    q = lax.broadcasted_iota(jnp.int32, (C2 * size_y, C2 * size_y), 1)
    from_row = (r % size_y) * C2 + r // size_y
    perm[...] = jnp.where(q == from_row, 1.0, 0.0).astype(BF16)
    acc1[...] = jnp.zeros_like(acc1)
    acc2[...] = jnp.zeros_like(acc2)
    tall3[...] = jnp.zeros_like(tall3)

    def over_space(body):
        def step(k, carry):
            body(k)
            return carry

        lax.fori_loop(1, n_space, step, 0)

    def arrive(group):
        for copy, (dx, dy) in zip(group, DIRS):
            @pl.when(there(-dx, -dy))
            def _():
                copy.wait_recv()

            @pl.when(there(dx, dy))
            def _():
                copy.wait_send()

    for k in range(1, n_samp):
        copy_1(k).wait()
    over_space(lambda k: copy_2(k).wait())
    m1 = gather_rows(all1, rows1, wide1)
    m2 = gather_rows(all2, rows2, wide2)
    base1 = jnp.concatenate([dot(m1, q1[kz]) for kz in range(3)], axis=0)
    base2 = jnp.concatenate([dot(m2, q2[kz]) for kz in range(3)], axis=0)
    for kx in range(3):
        for ky in range(3):
            first = 128 * kx + C2 * ky
            tall3[first : first + C2] = dot(m2, q3[3 * kx + ky])
    base3 = tall3[...].T[:48]
    for y in range(high_y):
        row = base1 if y == 0 else pltpu.roll(base1, 4 * y, axis=1)
        a1[48 * y : 48 * y + 48] = row[:, :192].astype(BF16)
    a2[:96] = base2[:, :192].astype(BF16)
    a2[96:] = pltpu.roll(base2, 16, axis=1)[:, :192].astype(BF16)
    a3[:48] = base3.astype(BF16)
    a3[48:] = pltpu.roll(base3, 32, axis=1).astype(BF16)

    arrive(vol)

    def lift(x, carry):
        for y in range(vp.shape[1]):
            vf[CIN * y : CIN * (y + 1)] = vp[x, y].astype(F32)
        vrows[x] = vf[...].astype(BF16)
        return carry

    lax.fori_loop(0, vp.shape[0], lift, 0)

    def vwin(x):
        return jnp.concatenate([vrows[x], vrows[x + 1], vrows[x + 2]], axis=0)

    def layer1(x, carry):
        gx = s * size_x + x - 2
        ok_x = (gx >= 0) & (gx < n_space * size_x)
        t1[...] = dot(a1[...], vwin(x))
        for y in range(high_y):
            gy = m * size_y + y - 2
            ok = ok_x & (gy >= 0) & (gy < n_samp * size_y)
            p = tap_sum(t1[48 * y : 48 * y + 48], C1, lane1, last)
            pre[x, 16 * y : 16 * y + 16] = p
            h = leaky(p) * jnp.where(ok, 1.0, 0.0)
            hid[x, 16 * y : 16 * y + 16] = h.astype(BF16)
        return carry

    lax.fori_loop(0, size_x + 4, layer1, 0)

    def hwin(x, y):
        return jnp.concatenate([hid[x + k, 16 * y : 16 * y + 64] for k in range(3)], axis=0)

    def pre_two(t, half):
        return tap_sum(t[96 * half : 96 * half + 96], C2, lane2, last)

    def back_two(x, y, p):
        b = (cp[x, y].astype(F32) * jnp.where(p > 0, 1.0, SLOPE)).astype(BF16)
        back[x, C2 * y : C2 * (y + 1)] = b
        return b

    def layer2(x, carry):
        moved, windows = [], []
        for y in range(1, 1 + size_y, 2):
            win = hwin(x + 1, y)
            t = dot(a2[...], win)
            both = []
            for half in range(2):
                p = pre_two(t, half)
                act[C2 * (y + half - 1) : C2 * (y + half)] = leaky(p).astype(BF16)
                b = back_two(x + 1, y + half, p)
                both.append(tap_spread(b.astype(F32), lane2, last).astype(BF16))
            moved.append(jnp.concatenate(both, axis=0))
            windows.append(win)
        acc2[...] += dot_nt(jnp.concatenate(moved, axis=1), jnp.concatenate(windows, axis=1))
        value = dot(perm[...], act[...])
        act_ref[:, x] = value.reshape(C2, size_y, size_z).astype(BF16)
        return carry

    lax.fori_loop(0, size_x, layer2, 0)

    def wide(values, rows):
        return jnp.concatenate([values, jnp.zeros((rows, 64), F32)], axis=1)

    def samp_peer(k):
        return lax.rem(m + k, n_samp)

    def space_peer(k):
        return lax.rem(s + k, n_space)

    def first_1(k):
        return pltpu.make_async_remote_copy(
            src_ref=grad1.at[samp_peer(k)], dst_ref=part1.at[m], send_sem=send_a1.at[k],
            recv_sem=recv_a1.at[k], device_id=(s, samp_peer(k)), device_id_type=MESH)

    def first_2(k):
        return pltpu.make_async_remote_copy(
            src_ref=grad2.at[space_peer(k)], dst_ref=part2.at[s], send_sem=send_a2.at[k],
            recv_sem=recv_a2.at[k], device_id=(space_peer(k), m), device_id_type=MESH)

    def second_1(k):
        return pltpu.make_async_remote_copy(
            src_ref=mine1, dst_ref=full1.at[s], send_sem=send_b1.at[k],
            recv_sem=recv_b1.at[k], device_id=(space_peer(k), m), device_id_type=MESH)

    def second_2(k):
        return pltpu.make_async_remote_copy(
            src_ref=mine2, dst_ref=full2.at[m], send_sem=send_b2.at[k],
            recv_sem=recv_b2.at[k], device_id=(s, samp_peer(k)), device_id_type=MESH)

    total2 = wide(acc2[:96], 96) + pltpu.roll(wide(acc2[96:], 96), 256 - 16, axis=1)
    scatter_rows(flat_order(total2, q2, C2), rows2, wide2, grad2)
    over_space(lambda k: first_2(k).start())
    part2[s] = grad2[s]

    arrive(cot)

    def edge_x(i, carry):
        x = (size_x + 1) * i
        for y in range(0, size_y + 2, 2):
            t = dot(a2[...], hwin(x, y))
            for half in range(2):
                back_two(x, y + half, pre_two(t, half))
        return carry

    lax.fori_loop(0, 2, edge_x, 0)

    def edge_y(x, carry):
        for half, y in ((0, 0), (1, size_y)):
            back_two(x + 1, y + half, pre_two(dot(a2[...], hwin(x + 1, y)), half))
        return carry

    lax.fori_loop(0, size_x, edge_y, 0)

    def finish(x, carry):
        pieces = []
        for y in range(0, size_y, 2):
            win = jnp.concatenate([back[x + k, C2 * y : C2 * y + 128] for k in range(3)], axis=0)
            t = dot(a3[...], win)
            for half in range(2):
                d = tap_sum(t[48 * half : 48 * half + 48], C1, lane1, last)
                p = pre[x + 2, 16 * (y + half + 2) : 16 * (y + half + 2) + 16]
                b1 = (d * jnp.where(p > 0, 1.0, SLOPE)).astype(BF16).astype(F32)
                pieces.append(tap_spread(b1, lane1, last).astype(BF16))
        acc1[...] += dot_nt(jnp.concatenate(pieces, axis=0), vwin(x + 2))
        return carry

    lax.fori_loop(0, size_x, finish, 0)

    total1 = jnp.zeros((48, 256), F32)
    for y in range(size_y):
        total1 = total1 + pltpu.roll(wide(acc1[48 * y : 48 * y + 48], 48), 256 - 4 * (y + 2), axis=1)
    scatter_rows(flat_order(total1, q1, C1), rows1, wide1, grad1)
    for k in range(1, n_samp):
        first_1(k).start()
    part1[m] = grad1[m]
    over_space(lambda k: first_2(k).wait())
    mine2[...] = jnp.sum(part2[...], axis=0)
    for k in range(1, n_samp):
        second_2(k).start()
    full2[m] = mine2[...]
    for k in range(1, n_samp):
        first_1(k).wait()
    mine1[...] = jnp.sum(part1[...], axis=0)
    over_space(lambda k: second_1(k).start())
    full1[s] = mine1[...]
    for k in range(1, n_samp):
        second_2(k).wait()
    o2_ref[...] = jnp.sum(full2[...], axis=0) * scale
    over_space(lambda k: second_1(k).wait())
    o1_ref[...] = jnp.sum(full1[...], axis=0) * scale


VMEM = pl.BlockSpec(memory_space=pltpu.VMEM)


def on_device(n_space, n_samp, volume, filters_one, filters_two, cotangent):
    _, size_x, size_y, size_z = volume.shape
    len1 = filters_one.shape[0]
    len2 = filters_two.shape[0]
    unit1 = math.gcd(len1, 27 * CIN)
    unit2 = math.gcd(len2, 27 * C1)
    piece1 = (len1 // unit1, unit1)
    piece2 = (len2 // unit2, unit2)
    high_y = size_y + 4
    scale = 1.0 / math.sqrt(float(size_x * n_space * size_y * n_samp * size_z))
    samp, space = pltpu.SemaphoreType.DMA((n_samp,)), pltpu.SemaphoreType.DMA((n_space,))
    sides = pltpu.SemaphoreType.DMA((8,))
    activation, out1, out2 = pl.pallas_call(
        functools.partial(fused_kernel, n_space, n_samp, scale),
        out_shape=[
            jax.ShapeDtypeStruct((C2, size_x, size_y, size_z), BF16),
            jax.ShapeDtypeStruct(piece1, F32),
            jax.ShapeDtypeStruct(piece2, F32),
        ],
        in_specs=[VMEM] * 4,
        out_specs=[VMEM] * 3,
        scratch_shapes=[
            pltpu.VMEM((size_x + 6, size_y + 8, CIN, size_z), BF16),
            pltpu.VMEM((size_x + 2, size_y + 2, C2, size_z), BF16),
            pltpu.VMEM((n_samp, *piece1), BF16),
            pltpu.VMEM((n_space, *piece2), BF16),
            pltpu.VMEM((48 * high_y, 192), BF16),
            pltpu.VMEM((192, 192), BF16),
            pltpu.VMEM((96, 384), BF16),
            pltpu.VMEM((size_x + 4, 16 * high_y, size_z), BF16),
            pltpu.VMEM((size_x + 2, C2 * (size_y + 2), size_z), BF16),
            pltpu.VMEM((size_x + 4, 16 * high_y, size_z), F32),
            pltpu.VMEM((48 * high_y, size_z), F32),
            pltpu.VMEM((C2 * size_y, C2 * size_y), BF16),
            pltpu.VMEM((48 * size_y, 192), F32),
            pltpu.VMEM((192, 192), F32),
            pltpu.VMEM((C2 * size_y, size_z), BF16),
            pltpu.VMEM((3, 27 * CIN, 256), BF16),
            pltpu.VMEM((3, 27 * C1, 256), BF16),
            pltpu.VMEM((9, 27 * C1, 128), BF16),
            pltpu.VMEM((n_samp * piece1[0], piece1[1]), F32),
            pltpu.VMEM((C1, 27 * CIN), F32),
            pltpu.VMEM((n_space * piece2[0], piece2[1]), F32),
            pltpu.VMEM((C2, 27 * C1), F32),
            pltpu.VMEM((384, 128), F32),
            pltpu.VMEM((CIN * (size_y + 8), size_z), F32),
            pltpu.VMEM((size_x + 6, CIN * (size_y + 8), size_z), BF16),
            pltpu.VMEM((n_samp, *piece1), F32),
            pltpu.VMEM((n_space, *piece2), F32),
            pltpu.VMEM((n_samp, *piece1), F32),
            pltpu.VMEM((n_space, *piece2), F32),
            pltpu.VMEM((n_space, *piece1), F32),
            pltpu.VMEM((n_samp, *piece2), F32),
            pltpu.VMEM(piece1, F32),
            pltpu.VMEM(piece2, F32),
            sides, sides, sides, sides, samp, samp, space, space,
            samp, samp, space, space, space, space, samp, samp,
        ],
        compiler_params=pltpu.CompilerParams(
            collective_id=0, has_side_effects=True, vmem_limit_bytes=48 * 2**20),
    )(volume.transpose(1, 2, 0, 3), cotangent.transpose(1, 2, 0, 3),
      filters_one.reshape(piece1), filters_two.reshape(piece2))
    return activation, out1.reshape(len1), out2.reshape(len2)


def solution(mesh):
    in_specs = (
        P(None, "space", "samp", None),
        P("samp"),
        P("space"),
        P(None, "space", "samp", None),
    )
    out_specs = (P(None, "space", "samp", None), P("samp"), P("space"))
    return jax.shard_map(
        functools.partial(on_device, mesh.shape["space"], mesh.shape["samp"]),
        mesh=mesh, in_specs=in_specs, out_specs=out_specs, check_vma=False,
    )
```

```python
import functools
import math

import jax
import jax.numpy as jnp
from jax import lax
from jax.experimental import pallas as pl
from jax.experimental.pallas import tpu as pltpu
from jax.sharding import PartitionSpec as P

CIN = 4
C1 = 16
C2 = 32
SLOPE = 0.3
MESH = pl.DeviceIdType.MESH
F32 = jnp.float32
BF16 = jnp.bfloat16
DIRS = [(dx, dy) for dx in (-1, 0, 1) for dy in (-1, 0, 1) if (dx, dy) != (0, 0)]


def spans(delta, size, width):
    if delta == 1:
        return (size - width, width), (0, width)
    if delta == -1:
        return (0, width), (size + width, width)
    return (0, size), (width, size)


def leaky(values):
    return jnp.where(values > 0, values, SLOPE * values)


def tap_sum(t, rows, lane, last):
    low = jnp.where(lane == 0, 0.0, pltpu.roll(t[:rows], 1, axis=1))
    high = jnp.where(lane == last, 0.0, pltpu.roll(t[2 * rows :], last, axis=1))
    return t[rows : 2 * rows] + low + high


def tap_spread(b, lane, last):
    low = jnp.where(lane == last, 0.0, pltpu.roll(b, last, axis=1))
    high = jnp.where(lane == 0, 0.0, pltpu.roll(b, 1, axis=1))
    return jnp.concatenate([low, b, high], axis=0)


def dot(a, b):
    return lax.dot_general(a, b, (((1,), (0,)), ((), ())), preferred_element_type=F32)


def dot_nt(a, b):
    return lax.dot_general(a, b, (((1,), (1,)), ((), ())), preferred_element_type=F32)


def one_hot(rows, source):
    row = lax.broadcasted_iota(jnp.int32, (rows, source.shape[1]), 0)
    return jnp.where(row == source, 1.0, 0.0).astype(BF16)


def one_hot_rows(chans, size_y):
    r = lax.broadcasted_iota(jnp.int32, (chans * size_y, chans * size_y), 0)
    q = lax.broadcasted_iota(jnp.int32, (chans * size_y, chans * size_y), 1)
    return jnp.where(q == (r % chans) * size_y + r // chans, 1.0, 0.0).astype(BF16)


def build_selectors(q1, q2, q3):
    lane = lax.broadcasted_iota(jnp.int32, (1, 256), 1)
    kx, ky, i = lane >> 6, (lane >> 2) & 15, lane & 3
    source1 = jnp.where((kx < 3) & (ky < 3), i * 27 + kx * 9 + ky * 3, -9)
    kx, ky, i = lane >> 6, (lane >> 4) & 3, lane & 15
    source2 = jnp.where((kx < 3) & (ky < 3), i * 27 + kx * 9 + ky * 3, -9)
    for kz in range(3):
        q1[kz] = one_hot(27 * CIN, source1 + kz)
        q2[kz] = one_hot(27 * C1, source2 + kz)
    lane = lax.broadcasted_iota(jnp.int32, (1, 128), 1)
    kz, i = lane >> 4, lane & 15
    for kx in range(3):
        for ky in range(3):
            source3 = jnp.where(kz < 3, i * 27 + (2 - kx) * 9 + (2 - ky) * 3 + 2 - kz, -9)
            q3[3 * kx + ky] = one_hot(27 * C1, source3)


def gather_rows(all_ref, rows_ref, wide_ref):
    owners, count, unit = all_ref.shape
    for j in range(owners):
        rows_ref[count * j : count * (j + 1)] = all_ref[j].astype(F32)
    split = wide_ref.shape[1] // unit
    if split == 1:
        return rows_ref[...].astype(BF16)
    for k in range(split):
        wide_ref[:, unit * k : unit * (k + 1)] = rows_ref[pl.ds(k, wide_ref.shape[0], stride=split)]
    return wide_ref[...].astype(BF16)


def scatter_rows(value, rows_ref, wide_ref, out_ref):
    owners, count, unit = out_ref.shape
    split = value.shape[1] // unit
    if split == 1:
        rows_ref[...] = value
    else:
        wide_ref[...] = value
        for k in range(split):
            rows_ref[pl.ds(k, value.shape[0], stride=split)] = wide_ref[:, unit * k : unit * (k + 1)]
    for j in range(owners):
        out_ref[j] = rows_ref[count * j : count * (j + 1)]


def flat_order(grad, q, chans):
    result = 0.0
    for kz in range(3):
        g = grad[chans * kz : chans * (kz + 1)]
        high = g.astype(BF16)
        rest = g - high.astype(F32)
        mid = rest.astype(BF16)
        low = (rest - mid.astype(F32)).astype(BF16)
        r = dot_nt(jnp.concatenate([high, mid, low], axis=0), q[kz])
        result = result + (r[:chans] + r[chans : 2 * chans] + r[2 * chans :])
    return result


def fused_kernel(
    n_space, n_samp, scale, v_ref, c_ref, f1_ref, f2_ref, act_ref, o1_ref, o2_ref,
    vp, cp, all1, all2,
    turn, a1, a2, a3, hid, back, pre, t1, perm, acc1, acc2, act,
    q1, q2, q3, rows1, wide1, rows2, wide2, tall3, vf, vrows,
    grad1, grad2, part1, part2, full1, full2, mine1, mine2,
    send_v, recv_v, send_c, recv_c, send_1, recv_1, send_2, recv_2,
    send_a1, recv_a1, send_a2, recv_a2, send_b1, recv_b1, send_b2, recv_b2,
):
    s = lax.axis_index("space")
    m = lax.axis_index("samp")
    size_x, size_y, size_z = v_ref.shape[1:]

    vp[...] = jnp.zeros_like(vp)

    def zero_row(x, carry):
        cp[x] = jnp.zeros(cp.shape[1:], cp.dtype)
        return carry

    lax.fori_loop(0, cp.shape[0], zero_row, 0)

    def there(dx, dy):
        return (s + dx >= 0) & (s + dx < n_space) & (m + dy >= 0) & (m + dy < n_samp)

    barrier = pltpu.get_barrier_semaphore()
    peers = n_samp - 1 + n_space - 1
    for dx, dy in DIRS:
        if dx == 0 or dy == 0:
            continue
        peers = peers + jnp.where(there(dx, dy), 1, 0)

        @pl.when(there(dx, dy))
        def _():
            pl.semaphore_signal(barrier, inc=1, device_id=(s + dx, m + dy), device_id_type=MESH)
    for k in range(1, n_samp):
        pl.semaphore_signal(barrier, inc=1, device_id=(s, lax.rem(m + k, n_samp)), device_id_type=MESH)

    def greet(k, carry):
        pl.semaphore_signal(barrier, inc=1, device_id=(lax.rem(s + k, n_space), m), device_id_type=MESH)
        return carry

    lax.fori_loop(1, n_space, greet, 0)

    turn[...] = one_hot_rows(C2, size_y)
    turn_v = one_hot_rows(CIN, size_y)

    def centre(x, carry):
        value = c_ref[:, x].astype(F32).reshape(C2 * size_y, size_z).astype(BF16)
        cp[x + 1, 1 : 1 + size_y] = dot(turn[...], value).astype(BF16).reshape(size_y, C2, size_z)
        value = v_ref[:, x].astype(F32).reshape(CIN * size_y, size_z).astype(BF16)
        value = dot(turn_v, value)
        for y in range(size_y):
            vp[x + 3, y + 3] = value[CIN * y : CIN * (y + 1)].astype(BF16)
        return carry

    lax.fori_loop(0, size_x, centre, 0)
    pl.semaphore_wait(barrier, peers)

    def copy_1(k):
        return pltpu.make_async_remote_copy(
            src_ref=f1_ref, dst_ref=all1.at[m], send_sem=send_1.at[k], recv_sem=recv_1.at[k],
            device_id=(s, lax.rem(m + k, n_samp)), device_id_type=MESH)

    def copy_2(k):
        return pltpu.make_async_remote_copy(
            src_ref=f2_ref, dst_ref=all2.at[s], send_sem=send_2.at[k], recv_sem=recv_2.at[k],
            device_id=(lax.rem(s + k, n_space), m), device_id_type=MESH)

    def halo(src, dst, width, send, recv, slot, dx, dy):
        (sx, nx), (tx, _) = spans(dx, size_x, width)
        (sy, ny), (ty, _) = spans(dy, size_y, width)
        return pltpu.make_async_remote_copy(
            src_ref=src.at[pl.ds(sx + width, nx), pl.ds(sy + width, ny)], dst_ref=dst.at[pl.ds(tx, nx), pl.ds(ty, ny)],
            send_sem=send.at[slot], recv_sem=recv.at[slot],
            device_id=(jnp.clip(s + dx, 0, n_space - 1), jnp.clip(m + dy, 0, n_samp - 1)),
            device_id_type=MESH)

    vol = [halo(vp, vp, 3, send_v, recv_v, j, dx, dy) for j, (dx, dy) in enumerate(DIRS)]
    cot = [halo(cp, cp, 1, send_c, recv_c, j, dx, dy) for j, (dx, dy) in enumerate(DIRS)]
    for k in range(1, n_samp):
        copy_1(k).start()

    def start_2(k, carry):
        copy_2(k).start()
        return carry

    lax.fori_loop(1, n_space, start_2, 0)
    for group in (vol, cot):
        for copy, (dx, dy) in zip(group, DIRS):
            @pl.when(there(dx, dy))
            def _():
                copy.start()

    all1[m] = f1_ref[...]
    all2[s] = f2_ref[...]
    last = size_z - 1
    high_y = size_y + 4

    def lanes(rows):
        return lax.broadcasted_iota(jnp.int32, (rows, size_z), 1)

    lane1 = lanes(C1)
    lane2 = lanes(C2)
    build_selectors(q1, q2, q3)
    r = lax.broadcasted_iota(jnp.int32, (C2 * size_y, C2 * size_y), 0)
    q = lax.broadcasted_iota(jnp.int32, (C2 * size_y, C2 * size_y), 1)
    from_row = (r % size_y) * C2 + r // size_y
    perm[...] = jnp.where(q == from_row, 1.0, 0.0).astype(BF16)
    acc1[...] = jnp.zeros_like(acc1)
    acc2[...] = jnp.zeros_like(acc2)
    tall3[...] = jnp.zeros_like(tall3)

    def over_space(body):
        def step(k, carry):
            body(k)
            return carry

        lax.fori_loop(1, n_space, step, 0)

    def arrive(group):
        for copy, (dx, dy) in zip(group, DIRS):
            @pl.when(there(-dx, -dy))
            def _():
                copy.wait_recv()

            @pl.when(there(dx, dy))
            def _():
                copy.wait_send()

    for k in range(1, n_samp):
        copy_1(k).wait()
    over_space(lambda k: copy_2(k).wait())
    m1 = gather_rows(all1, rows1, wide1)
    m2 = gather_rows(all2, rows2, wide2)
    base1 = jnp.concatenate([dot(m1, q1[kz]) for kz in range(3)], axis=0)
    base2 = jnp.concatenate([dot(m2, q2[kz]) for kz in range(3)], axis=0)
    for kx in range(3):
        for ky in range(3):
            first = 128 * kx + C2 * ky
            tall3[first : first + C2] = dot(m2, q3[3 * kx + ky])
    base3 = tall3[...].T[:48]
    for y in range(high_y):
        row = base1 if y == 0 else pltpu.roll(base1, 4 * y, axis=1)
        a1[48 * y : 48 * y + 48] = row[:, :192].astype(BF16)
    a2[:96] = base2[:, :192].astype(BF16)
    a2[96:] = pltpu.roll(base2, 16, axis=1)[:, :192].astype(BF16)
    a3[:48] = base3.astype(BF16)
    a3[48:] = pltpu.roll(base3, 32, axis=1).astype(BF16)

    arrive(vol)

    def lift(x, carry):
        for y in range(vp.shape[1]):
            vf[CIN * y : CIN * (y + 1)] = vp[x, y].astype(F32)
        vrows[x] = vf[...].astype(BF16)
        return carry

    lax.fori_loop(0, vp.shape[0], lift, 0)

    def vwin(x):
        return jnp.concatenate([vrows[x], vrows[x + 1], vrows[x + 2]], axis=0)

    def layer1(x, carry):
        gx = s * size_x + x - 2
        ok_x = (gx >= 0) & (gx < n_space * size_x)
        t1[...] = dot(a1[...], vwin(x))
        for y in range(high_y):
            gy = m * size_y + y - 2
            ok = ok_x & (gy >= 0) & (gy < n_samp * size_y)
            p = tap_sum(t1[48 * y : 48 * y + 48], C1, lane1, last)
            pre[x, 16 * y : 16 * y + 16] = p
            h = leaky(p) * jnp.where(ok, 1.0, 0.0)
            hid[x, 16 * y : 16 * y + 16] = h.astype(BF16)
        return carry

    lax.fori_loop(0, size_x + 4, layer1, 0)

    def hwin(x, y):
        return jnp.concatenate([hid[x + k, 16 * y : 16 * y + 64] for k in range(3)], axis=0)

    def pre_two(t, half):
        return tap_sum(t[96 * half : 96 * half + 96], C2, lane2, last)

    def back_two(x, y, p):
        b = (cp[x, y].astype(F32) * jnp.where(p > 0, 1.0, SLOPE)).astype(BF16)
        back[x, C2 * y : C2 * (y + 1)] = b
        return b

    def layer2(x, carry):
        moved, windows = [], []
        for y in range(1, 1 + size_y, 2):
            win = hwin(x + 1, y)
            t = dot(a2[...], win)
            both = []
            for half in range(2):
                p = pre_two(t, half)
                act[C2 * (y + half - 1) : C2 * (y + half)] = leaky(p).astype(BF16)
                b = back_two(x + 1, y + half, p)
                both.append(tap_spread(b.astype(F32), lane2, last).astype(BF16))
            moved.append(jnp.concatenate(both, axis=0))
            windows.append(win)
        acc2[...] += dot_nt(jnp.concatenate(moved, axis=1), jnp.concatenate(windows, axis=1))
        value = dot(perm[...], act[...])
        act_ref[:, x] = value.reshape(C2, size_y, size_z).astype(BF16)
        return carry

    lax.fori_loop(0, size_x, layer2, 0)

    def wide(values, rows):
        return jnp.concatenate([values, jnp.zeros((rows, 64), F32)], axis=1)

    def samp_peer(k):
        return lax.rem(m + k, n_samp)

    def space_peer(k):
        return lax.rem(s + k, n_space)

    def first_1(k):
        return pltpu.make_async_remote_copy(
            src_ref=grad1.at[samp_peer(k)], dst_ref=part1.at[m], send_sem=send_a1.at[k],
            recv_sem=recv_a1.at[k], device_id=(s, samp_peer(k)), device_id_type=MESH)

    def first_2(k):
        return pltpu.make_async_remote_copy(
            src_ref=grad2.at[space_peer(k)], dst_ref=part2.at[s], send_sem=send_a2.at[k],
            recv_sem=recv_a2.at[k], device_id=(space_peer(k), m), device_id_type=MESH)

    def second_1(k):
        return pltpu.make_async_remote_copy(
            src_ref=mine1, dst_ref=full1.at[s], send_sem=send_b1.at[k],
            recv_sem=recv_b1.at[k], device_id=(space_peer(k), m), device_id_type=MESH)

    def second_2(k):
        return pltpu.make_async_remote_copy(
            src_ref=mine2, dst_ref=full2.at[m], send_sem=send_b2.at[k],
            recv_sem=recv_b2.at[k], device_id=(s, samp_peer(k)), device_id_type=MESH)

    total2 = wide(acc2[:96], 96) + pltpu.roll(wide(acc2[96:], 96), 256 - 16, axis=1)
    scatter_rows(flat_order(total2, q2, C2), rows2, wide2, grad2)
    over_space(lambda k: first_2(k).start())
    part2[s] = grad2[s]

    arrive(cot)

    def edge_x(i, carry):
        x = (size_x + 1) * i
        for y in range(0, size_y + 2, 2):
            t = dot(a2[...], hwin(x, y))
            for half in range(2):
                back_two(x, y + half, pre_two(t, half))
        return carry

    lax.fori_loop(0, 2, edge_x, 0)

    def edge_y(x, carry):
        for half, y in ((0, 0), (1, size_y)):
            back_two(x + 1, y + half, pre_two(dot(a2[...], hwin(x + 1, y)), half))
        return carry

    lax.fori_loop(0, size_x, edge_y, 0)

    def finish(x, carry):
        pieces = []
        for y in range(0, size_y, 2):
            win = jnp.concatenate([back[x + k, C2 * y : C2 * y + 128] for k in range(3)], axis=0)
            t = dot(a3[...], win)
            for half in range(2):
                d = tap_sum(t[48 * half : 48 * half + 48], C1, lane1, last)
                p = pre[x + 2, 16 * (y + half + 2) : 16 * (y + half + 2) + 16]
                b1 = (d * jnp.where(p > 0, 1.0, SLOPE)).astype(BF16).astype(F32)
                pieces.append(tap_spread(b1, lane1, last).astype(BF16))
        acc1[...] += dot_nt(jnp.concatenate(pieces, axis=0), vwin(x + 2))
        return carry

    lax.fori_loop(0, size_x, finish, 0)

    total1 = jnp.zeros((48, 256), F32)
    for y in range(size_y):
        total1 = total1 + pltpu.roll(wide(acc1[48 * y : 48 * y + 48], 48), 256 - 4 * (y + 2), axis=1)
    scatter_rows(flat_order(total1, q1, C1), rows1, wide1, grad1)
    for k in range(1, n_samp):
        first_1(k).start()
    part1[m] = grad1[m]
    over_space(lambda k: first_2(k).wait())
    mine2[...] = jnp.sum(part2[...], axis=0)
    for k in range(1, n_samp):
        second_2(k).start()
    full2[m] = mine2[...]
    for k in range(1, n_samp):
        first_1(k).wait()
    mine1[...] = jnp.sum(part1[...], axis=0)
    over_space(lambda k: second_1(k).start())
    full1[s] = mine1[...]
    for k in range(1, n_samp):
        second_2(k).wait()
    o2_ref[...] = jnp.sum(full2[...], axis=0) * scale
    over_space(lambda k: second_1(k).wait())
    o1_ref[...] = jnp.sum(full1[...], axis=0) * scale


VMEM = pl.BlockSpec(memory_space=pltpu.VMEM)


def on_device(n_space, n_samp, volume, filters_one, filters_two, cotangent):
    _, size_x, size_y, size_z = volume.shape
    len1 = filters_one.shape[0]
    len2 = filters_two.shape[0]
    unit1 = math.gcd(len1, 27 * CIN)
    unit2 = math.gcd(len2, 27 * C1)
    piece1 = (len1 // unit1, unit1)
    piece2 = (len2 // unit2, unit2)
    high_y = size_y + 4
    scale = 1.0 / math.sqrt(float(size_x * n_space * size_y * n_samp * size_z))
    samp, space = pltpu.SemaphoreType.DMA((n_samp,)), pltpu.SemaphoreType.DMA((n_space,))
    sides = pltpu.SemaphoreType.DMA((8,))
    activation, out1, out2 = pl.pallas_call(
        functools.partial(fused_kernel, n_space, n_samp, scale),
        out_shape=[
            jax.ShapeDtypeStruct((C2, size_x, size_y, size_z), BF16),
            jax.ShapeDtypeStruct(piece1, F32),
            jax.ShapeDtypeStruct(piece2, F32),
        ],
        in_specs=[VMEM] * 4,
        out_specs=[VMEM] * 3,
        scratch_shapes=[
            pltpu.VMEM((size_x + 6, size_y + 8, CIN, size_z), BF16),
            pltpu.VMEM((size_x + 2, size_y + 2, C2, size_z), BF16),
            pltpu.VMEM((n_samp, *piece1), BF16),
            pltpu.VMEM((n_space, *piece2), BF16),
            pltpu.VMEM((C2 * size_y, C2 * size_y), BF16),
            pltpu.VMEM((48 * high_y, 192), BF16),
            pltpu.VMEM((192, 192), BF16),
            pltpu.VMEM((96, 384), BF16),
            pltpu.VMEM((size_x + 4, 16 * high_y, size_z), BF16),
            pltpu.VMEM((size_x + 2, C2 * (size_y + 2), size_z), BF16),
            pltpu.VMEM((size_x + 4, 16 * high_y, size_z), F32),
            pltpu.VMEM((48 * high_y, size_z), F32),
            pltpu.VMEM((C2 * size_y, C2 * size_y), BF16),
            pltpu.VMEM((48 * size_y, 192), F32),
            pltpu.VMEM((192, 192), F32),
            pltpu.VMEM((C2 * size_y, size_z), BF16),
            pltpu.VMEM((3, 27 * CIN, 256), BF16),
            pltpu.VMEM((3, 27 * C1, 256), BF16),
            pltpu.VMEM((9, 27 * C1, 128), BF16),
            pltpu.VMEM((n_samp * piece1[0], piece1[1]), F32),
            pltpu.VMEM((C1, 27 * CIN), F32),
            pltpu.VMEM((n_space * piece2[0], piece2[1]), F32),
            pltpu.VMEM((C2, 27 * C1), F32),
            pltpu.VMEM((384, 128), F32),
            pltpu.VMEM((CIN * (size_y + 8), size_z), F32),
            pltpu.VMEM((size_x + 6, CIN * (size_y + 8), size_z), BF16),
            pltpu.VMEM((n_samp, *piece1), F32),
            pltpu.VMEM((n_space, *piece2), F32),
            pltpu.VMEM((n_samp, *piece1), F32),
            pltpu.VMEM((n_space, *piece2), F32),
            pltpu.VMEM((n_space, *piece1), F32),
            pltpu.VMEM((n_samp, *piece2), F32),
            pltpu.VMEM(piece1, F32),
            pltpu.VMEM(piece2, F32),
            sides, sides, sides, sides, samp, samp, space, space,
            samp, samp, space, space, space, space, samp, samp,
        ],
        compiler_params=pltpu.CompilerParams(
            collective_id=0, has_side_effects=True, vmem_limit_bytes=48 * 2**20),
    )(volume, cotangent,
      filters_one.reshape(piece1), filters_two.reshape(piece2))
    return activation, out1.reshape(len1), out2.reshape(len2)


def solution(mesh):
    in_specs = (
        P(None, "space", "samp", None),
        P("samp"),
        P("space"),
        P(None, "space", "samp", None),
    )
    out_specs = (P(None, "space", "samp", None), P("samp"), P("space"))
    return jax.shard_map(
        functools.partial(on_device, mesh.shape["space"], mesh.shape["samp"]),
        mesh=mesh, in_specs=in_specs, out_specs=out_specs, check_vma=False,
    )
```

```python
import functools
import math

import jax
import jax.numpy as jnp
from jax import lax
from jax.experimental import pallas as pl
from jax.experimental.pallas import tpu as pltpu
from jax.sharding import PartitionSpec as P

CIN = 4
C1 = 16
C2 = 32
SLOPE = 0.3
MESH = pl.DeviceIdType.MESH
F32 = jnp.float32
BF16 = jnp.bfloat16
DIRS = [(dx, dy) for dx in (-1, 0, 1) for dy in (-1, 0, 1) if (dx, dy) != (0, 0)]


def spans(delta, size, width):
    if delta == 1:
        return (size - width, width), (0, width)
    if delta == -1:
        return (0, width), (size + width, width)
    return (0, size), (width, size)


def leaky(values):
    return jnp.where(values > 0, values, SLOPE * values)


def tap_sum(t, rows, lane, last):
    low = jnp.where(lane == 0, 0.0, pltpu.roll(t[:rows], 1, axis=1))
    high = jnp.where(lane == last, 0.0, pltpu.roll(t[2 * rows :], last, axis=1))
    return t[rows : 2 * rows] + low + high


def tap_spread(b, lane, last):
    low = jnp.where(lane == last, 0.0, pltpu.roll(b, last, axis=1))
    high = jnp.where(lane == 0, 0.0, pltpu.roll(b, 1, axis=1))
    return jnp.concatenate([low, b, high], axis=0)


def dot(a, b):
    return lax.dot_general(a, b, (((1,), (0,)), ((), ())), preferred_element_type=F32)


def dot_nt(a, b):
    return lax.dot_general(a, b, (((1,), (1,)), ((), ())), preferred_element_type=F32)


def one_hot(rows, source):
    row = lax.broadcasted_iota(jnp.int32, (rows, source.shape[1]), 0)
    return jnp.where(row == source, 1.0, 0.0).astype(BF16)


def one_hot_rows(chans, size_y):
    r = lax.broadcasted_iota(jnp.int32, (chans * size_y, chans * size_y), 0)
    q = lax.broadcasted_iota(jnp.int32, (chans * size_y, chans * size_y), 1)
    return jnp.where(q == (r % chans) * size_y + r // chans, 1.0, 0.0).astype(BF16)


def build_selectors(q1, q2, q3):
    lane = lax.broadcasted_iota(jnp.int32, (1, 256), 1)
    kx, ky, i = lane >> 6, (lane >> 2) & 15, lane & 3
    source1 = jnp.where((kx < 3) & (ky < 3), i * 27 + kx * 9 + ky * 3, -9)
    kx, ky, i = lane >> 6, (lane >> 4) & 3, lane & 15
    source2 = jnp.where((kx < 3) & (ky < 3), i * 27 + kx * 9 + ky * 3, -9)
    for kz in range(3):
        q1[kz] = one_hot(27 * CIN, source1 + kz)
        q2[kz] = one_hot(27 * C1, source2 + kz)
    lane = lax.broadcasted_iota(jnp.int32, (1, 128), 1)
    kz, i = lane >> 4, lane & 15
    for kx in range(3):
        for ky in range(3):
            source3 = jnp.where(kz < 3, i * 27 + (2 - kx) * 9 + (2 - ky) * 3 + 2 - kz, -9)
            q3[3 * kx + ky] = one_hot(27 * C1, source3)


def gather_rows(all_ref, rows_ref, wide_ref):
    owners, count, unit = all_ref.shape
    for j in range(owners):
        rows_ref[count * j : count * (j + 1)] = all_ref[j].astype(F32)
    split = wide_ref.shape[1] // unit
    if split == 1:
        return rows_ref[...].astype(BF16)
    for k in range(split):
        wide_ref[:, unit * k : unit * (k + 1)] = rows_ref[pl.ds(k, wide_ref.shape[0], stride=split)]
    return wide_ref[...].astype(BF16)


def scatter_rows(value, rows_ref, wide_ref, out_ref):
    owners, count, unit = out_ref.shape
    split = value.shape[1] // unit
    if split == 1:
        rows_ref[...] = value
    else:
        wide_ref[...] = value
        for k in range(split):
            rows_ref[pl.ds(k, value.shape[0], stride=split)] = wide_ref[:, unit * k : unit * (k + 1)]
    for j in range(owners):
        out_ref[j] = rows_ref[count * j : count * (j + 1)]


def flat_order(grad, q, chans):
    result = 0.0
    for kz in range(3):
        g = grad[chans * kz : chans * (kz + 1)]
        high = g.astype(BF16)
        rest = g - high.astype(F32)
        mid = rest.astype(BF16)
        low = (rest - mid.astype(F32)).astype(BF16)
        r = dot_nt(jnp.concatenate([high, mid, low], axis=0), q[kz])
        result = result + (r[:chans] + r[chans : 2 * chans] + r[2 * chans :])
    return result


def fused_kernel(
    n_space, n_samp, scale, v_hbm, c_hbm, f1_ref, f2_ref, act_ref, o1_ref, o2_ref,
    vp, cp, all1, all2,
    v_ref, c_ref, load_v, load_c, turn, a1, a2, a3, hid, back, pre, t1, perm, acc1, acc2, act,
    q1, q2, q3, rows1, wide1, rows2, wide2, tall3, vf, vrows,
    grad1, grad2, part1, part2, full1, full2, mine1, mine2,
    send_v, recv_v, send_c, recv_c, send_1, recv_1, send_2, recv_2,
    send_a1, recv_a1, send_a2, recv_a2, send_b1, recv_b1, send_b2, recv_b2,
):
    s = lax.axis_index("space")
    m = lax.axis_index("samp")
    size_x, size_y, size_z = v_ref.shape[1:]
    loads = [pltpu.make_async_copy(v_hbm, v_ref, load_v), pltpu.make_async_copy(c_hbm, c_ref, load_c)]
    for load in loads:
        load.start()

    vp[...] = jnp.zeros_like(vp)

    def zero_row(x, carry):
        cp[x] = jnp.zeros(cp.shape[1:], cp.dtype)
        return carry

    lax.fori_loop(0, cp.shape[0], zero_row, 0)

    def there(dx, dy):
        return (s + dx >= 0) & (s + dx < n_space) & (m + dy >= 0) & (m + dy < n_samp)

    barrier = pltpu.get_barrier_semaphore()
    peers = n_samp - 1 + n_space - 1
    for dx, dy in DIRS:
        if dx == 0 or dy == 0:
            continue
        peers = peers + jnp.where(there(dx, dy), 1, 0)

        @pl.when(there(dx, dy))
        def _():
            pl.semaphore_signal(barrier, inc=1, device_id=(s + dx, m + dy), device_id_type=MESH)
    for k in range(1, n_samp):
        pl.semaphore_signal(barrier, inc=1, device_id=(s, lax.rem(m + k, n_samp)), device_id_type=MESH)

    def greet(k, carry):
        pl.semaphore_signal(barrier, inc=1, device_id=(lax.rem(s + k, n_space), m), device_id_type=MESH)
        return carry

    lax.fori_loop(1, n_space, greet, 0)

    turn[...] = one_hot_rows(C2, size_y)
    turn_v = one_hot_rows(CIN, size_y)

    for load in loads:
        load.wait()

    def centre(x, carry):
        value = c_ref[:, x].astype(F32).reshape(C2 * size_y, size_z).astype(BF16)
        cp[x + 1, 1 : 1 + size_y] = dot(turn[...], value).astype(BF16).reshape(size_y, C2, size_z)
        value = v_ref[:, x].astype(F32).reshape(CIN * size_y, size_z).astype(BF16)
        value = dot(turn_v, value)
        for y in range(size_y):
            vp[x + 3, y + 3] = value[CIN * y : CIN * (y + 1)].astype(BF16)
        return carry

    lax.fori_loop(0, size_x, centre, 0)
    pl.semaphore_wait(barrier, peers)

    def copy_1(k):
        return pltpu.make_async_remote_copy(
            src_ref=f1_ref, dst_ref=all1.at[m], send_sem=send_1.at[k], recv_sem=recv_1.at[k],
            device_id=(s, lax.rem(m + k, n_samp)), device_id_type=MESH)

    def copy_2(k):
        return pltpu.make_async_remote_copy(
            src_ref=f2_ref, dst_ref=all2.at[s], send_sem=send_2.at[k], recv_sem=recv_2.at[k],
            device_id=(lax.rem(s + k, n_space), m), device_id_type=MESH)

    def halo(src, dst, width, send, recv, slot, dx, dy):
        (sx, nx), (tx, _) = spans(dx, size_x, width)
        (sy, ny), (ty, _) = spans(dy, size_y, width)
        return pltpu.make_async_remote_copy(
            src_ref=src.at[pl.ds(sx + width, nx), pl.ds(sy + width, ny)], dst_ref=dst.at[pl.ds(tx, nx), pl.ds(ty, ny)],
            send_sem=send.at[slot], recv_sem=recv.at[slot],
            device_id=(jnp.clip(s + dx, 0, n_space - 1), jnp.clip(m + dy, 0, n_samp - 1)),
            device_id_type=MESH)

    vol = [halo(vp, vp, 3, send_v, recv_v, j, dx, dy) for j, (dx, dy) in enumerate(DIRS)]
    cot = [halo(cp, cp, 1, send_c, recv_c, j, dx, dy) for j, (dx, dy) in enumerate(DIRS)]
    for k in range(1, n_samp):
        copy_1(k).start()

    def start_2(k, carry):
        copy_2(k).start()
        return carry

    lax.fori_loop(1, n_space, start_2, 0)
    for group in (vol, cot):
        for copy, (dx, dy) in zip(group, DIRS):
            @pl.when(there(dx, dy))
            def _():
                copy.start()

    all1[m] = f1_ref[...]
    all2[s] = f2_ref[...]
    last = size_z - 1
    high_y = size_y + 4

    def lanes(rows):
        return lax.broadcasted_iota(jnp.int32, (rows, size_z), 1)

    lane1 = lanes(C1)
    lane2 = lanes(C2)
    build_selectors(q1, q2, q3)
    r = lax.broadcasted_iota(jnp.int32, (C2 * size_y, C2 * size_y), 0)
    q = lax.broadcasted_iota(jnp.int32, (C2 * size_y, C2 * size_y), 1)
    from_row = (r % size_y) * C2 + r // size_y
    perm[...] = jnp.where(q == from_row, 1.0, 0.0).astype(BF16)
    acc1[...] = jnp.zeros_like(acc1)
    acc2[...] = jnp.zeros_like(acc2)
    tall3[...] = jnp.zeros_like(tall3)

    def over_space(body):
        def step(k, carry):
            body(k)
            return carry

        lax.fori_loop(1, n_space, step, 0)

    def arrive(group):
        for copy, (dx, dy) in zip(group, DIRS):
            @pl.when(there(-dx, -dy))
            def _():
                copy.wait_recv()

            @pl.when(there(dx, dy))
            def _():
                copy.wait_send()

    for k in range(1, n_samp):
        copy_1(k).wait()
    over_space(lambda k: copy_2(k).wait())
    m1 = gather_rows(all1, rows1, wide1)
    m2 = gather_rows(all2, rows2, wide2)
    base1 = jnp.concatenate([dot(m1, q1[kz]) for kz in range(3)], axis=0)
    base2 = jnp.concatenate([dot(m2, q2[kz]) for kz in range(3)], axis=0)
    for kx in range(3):
        for ky in range(3):
            first = 128 * kx + C2 * ky
            tall3[first : first + C2] = dot(m2, q3[3 * kx + ky])
    base3 = tall3[...].T[:48]
    for y in range(high_y):
        row = base1 if y == 0 else pltpu.roll(base1, 4 * y, axis=1)
        a1[48 * y : 48 * y + 48] = row[:, :192].astype(BF16)
    a2[:96] = base2[:, :192].astype(BF16)
    a2[96:] = pltpu.roll(base2, 16, axis=1)[:, :192].astype(BF16)
    a3[:48] = base3.astype(BF16)
    a3[48:] = pltpu.roll(base3, 32, axis=1).astype(BF16)

    arrive(vol)

    def lift(x, carry):
        for y in range(vp.shape[1]):
            vf[CIN * y : CIN * (y + 1)] = vp[x, y].astype(F32)
        vrows[x] = vf[...].astype(BF16)
        return carry

    lax.fori_loop(0, vp.shape[0], lift, 0)

    def vwin(x):
        return jnp.concatenate([vrows[x], vrows[x + 1], vrows[x + 2]], axis=0)

    def layer1(x, carry):
        gx = s * size_x + x - 2
        ok_x = (gx >= 0) & (gx < n_space * size_x)
        t1[...] = dot(a1[...], vwin(x))
        for y in range(high_y):
            gy = m * size_y + y - 2
            ok = ok_x & (gy >= 0) & (gy < n_samp * size_y)
            p = tap_sum(t1[48 * y : 48 * y + 48], C1, lane1, last)
            pre[x, 16 * y : 16 * y + 16] = p
            h = leaky(p) * jnp.where(ok, 1.0, 0.0)
            hid[x, 16 * y : 16 * y + 16] = h.astype(BF16)
        return carry

    lax.fori_loop(0, size_x + 4, layer1, 0)

    def hwin(x, y):
        return jnp.concatenate([hid[x + k, 16 * y : 16 * y + 64] for k in range(3)], axis=0)

    def pre_two(t, half):
        return tap_sum(t[96 * half : 96 * half + 96], C2, lane2, last)

    def back_two(x, y, p):
        b = (cp[x, y].astype(F32) * jnp.where(p > 0, 1.0, SLOPE)).astype(BF16)
        back[x, C2 * y : C2 * (y + 1)] = b
        return b

    def layer2(x, carry):
        moved, windows = [], []
        for y in range(1, 1 + size_y, 2):
            win = hwin(x + 1, y)
            t = dot(a2[...], win)
            both = []
            for half in range(2):
                p = pre_two(t, half)
                act[C2 * (y + half - 1) : C2 * (y + half)] = leaky(p).astype(BF16)
                b = back_two(x + 1, y + half, p)
                both.append(tap_spread(b.astype(F32), lane2, last).astype(BF16))
            moved.append(jnp.concatenate(both, axis=0))
            windows.append(win)
        acc2[...] += dot_nt(jnp.concatenate(moved, axis=1), jnp.concatenate(windows, axis=1))
        value = dot(perm[...], act[...])
        act_ref[:, x] = value.reshape(C2, size_y, size_z).astype(BF16)
        return carry

    lax.fori_loop(0, size_x, layer2, 0)

    def wide(values, rows):
        return jnp.concatenate([values, jnp.zeros((rows, 64), F32)], axis=1)

    def samp_peer(k):
        return lax.rem(m + k, n_samp)

    def space_peer(k):
        return lax.rem(s + k, n_space)

    def first_1(k):
        return pltpu.make_async_remote_copy(
            src_ref=grad1.at[samp_peer(k)], dst_ref=part1.at[m], send_sem=send_a1.at[k],
            recv_sem=recv_a1.at[k], device_id=(s, samp_peer(k)), device_id_type=MESH)

    def first_2(k):
        return pltpu.make_async_remote_copy(
            src_ref=grad2.at[space_peer(k)], dst_ref=part2.at[s], send_sem=send_a2.at[k],
            recv_sem=recv_a2.at[k], device_id=(space_peer(k), m), device_id_type=MESH)

    def second_1(k):
        return pltpu.make_async_remote_copy(
            src_ref=mine1, dst_ref=full1.at[s], send_sem=send_b1.at[k],
            recv_sem=recv_b1.at[k], device_id=(space_peer(k), m), device_id_type=MESH)

    def second_2(k):
        return pltpu.make_async_remote_copy(
            src_ref=mine2, dst_ref=full2.at[m], send_sem=send_b2.at[k],
            recv_sem=recv_b2.at[k], device_id=(s, samp_peer(k)), device_id_type=MESH)

    total2 = wide(acc2[:96], 96) + pltpu.roll(wide(acc2[96:], 96), 256 - 16, axis=1)
    scatter_rows(flat_order(total2, q2, C2), rows2, wide2, grad2)
    over_space(lambda k: first_2(k).start())
    part2[s] = grad2[s]

    arrive(cot)

    def edge_x(i, carry):
        x = (size_x + 1) * i
        for y in range(0, size_y + 2, 2):
            t = dot(a2[...], hwin(x, y))
            for half in range(2):
                back_two(x, y + half, pre_two(t, half))
        return carry

    lax.fori_loop(0, 2, edge_x, 0)

    def edge_y(x, carry):
        for half, y in ((0, 0), (1, size_y)):
            back_two(x + 1, y + half, pre_two(dot(a2[...], hwin(x + 1, y)), half))
        return carry

    lax.fori_loop(0, size_x, edge_y, 0)

    def finish(x, carry):
        pieces = []
        for y in range(0, size_y, 2):
            win = jnp.concatenate([back[x + k, C2 * y : C2 * y + 128] for k in range(3)], axis=0)
            t = dot(a3[...], win)
            for half in range(2):
                d = tap_sum(t[48 * half : 48 * half + 48], C1, lane1, last)
                p = pre[x + 2, 16 * (y + half + 2) : 16 * (y + half + 2) + 16]
                b1 = (d * jnp.where(p > 0, 1.0, SLOPE)).astype(BF16).astype(F32)
                pieces.append(tap_spread(b1, lane1, last).astype(BF16))
        acc1[...] += dot_nt(jnp.concatenate(pieces, axis=0), vwin(x + 2))
        return carry

    lax.fori_loop(0, size_x, finish, 0)

    total1 = jnp.zeros((48, 256), F32)
    for y in range(size_y):
        total1 = total1 + pltpu.roll(wide(acc1[48 * y : 48 * y + 48], 48), 256 - 4 * (y + 2), axis=1)
    scatter_rows(flat_order(total1, q1, C1), rows1, wide1, grad1)
    for k in range(1, n_samp):
        first_1(k).start()
    part1[m] = grad1[m]
    over_space(lambda k: first_2(k).wait())
    mine2[...] = jnp.sum(part2[...], axis=0)
    for k in range(1, n_samp):
        second_2(k).start()
    full2[m] = mine2[...]
    for k in range(1, n_samp):
        first_1(k).wait()
    mine1[...] = jnp.sum(part1[...], axis=0)
    over_space(lambda k: second_1(k).start())
    full1[s] = mine1[...]
    for k in range(1, n_samp):
        second_2(k).wait()
    o2_ref[...] = jnp.sum(full2[...], axis=0) * scale
    over_space(lambda k: second_1(k).wait())
    o1_ref[...] = jnp.sum(full1[...], axis=0) * scale


VMEM = pl.BlockSpec(memory_space=pltpu.VMEM)
HBM = pl.BlockSpec(memory_space=pltpu.HBM)


def on_device(n_space, n_samp, volume, filters_one, filters_two, cotangent):
    _, size_x, size_y, size_z = volume.shape
    len1 = filters_one.shape[0]
    len2 = filters_two.shape[0]
    unit1 = math.gcd(len1, 27 * CIN)
    unit2 = math.gcd(len2, 27 * C1)
    piece1 = (len1 // unit1, unit1)
    piece2 = (len2 // unit2, unit2)
    high_y = size_y + 4
    scale = 1.0 / math.sqrt(float(size_x * n_space * size_y * n_samp * size_z))
    samp, space = pltpu.SemaphoreType.DMA((n_samp,)), pltpu.SemaphoreType.DMA((n_space,))
    sides = pltpu.SemaphoreType.DMA((8,))
    activation, out1, out2 = pl.pallas_call(
        functools.partial(fused_kernel, n_space, n_samp, scale),
        out_shape=[
            jax.ShapeDtypeStruct((C2, size_x, size_y, size_z), BF16),
            jax.ShapeDtypeStruct(piece1, F32),
            jax.ShapeDtypeStruct(piece2, F32),
        ],
        in_specs=[HBM, HBM, VMEM, VMEM],
        out_specs=[VMEM] * 3,
        scratch_shapes=[
            pltpu.VMEM((size_x + 6, size_y + 8, CIN, size_z), BF16),
            pltpu.VMEM((size_x + 2, size_y + 2, C2, size_z), BF16),
            pltpu.VMEM((n_samp, *piece1), BF16),
            pltpu.VMEM((n_space, *piece2), BF16),
            pltpu.VMEM(volume.shape, BF16),
            pltpu.VMEM(cotangent.shape, BF16),
            pltpu.SemaphoreType.DMA(()),
            pltpu.SemaphoreType.DMA(()),
            pltpu.VMEM((C2 * size_y, C2 * size_y), BF16),
            pltpu.VMEM((48 * high_y, 192), BF16),
            pltpu.VMEM((192, 192), BF16),
            pltpu.VMEM((96, 384), BF16),
            pltpu.VMEM((size_x + 4, 16 * high_y, size_z), BF16),
            pltpu.VMEM((size_x + 2, C2 * (size_y + 2), size_z), BF16),
            pltpu.VMEM((size_x + 4, 16 * high_y, size_z), F32),
            pltpu.VMEM((48 * high_y, size_z), F32),
            pltpu.VMEM((C2 * size_y, C2 * size_y), BF16),
            pltpu.VMEM((48 * size_y, 192), F32),
            pltpu.VMEM((192, 192), F32),
            pltpu.VMEM((C2 * size_y, size_z), BF16),
            pltpu.VMEM((3, 27 * CIN, 256), BF16),
            pltpu.VMEM((3, 27 * C1, 256), BF16),
            pltpu.VMEM((9, 27 * C1, 128), BF16),
            pltpu.VMEM((n_samp * piece1[0], piece1[1]), F32),
            pltpu.VMEM((C1, 27 * CIN), F32),
            pltpu.VMEM((n_space * piece2[0], piece2[1]), F32),
            pltpu.VMEM((C2, 27 * C1), F32),
            pltpu.VMEM((384, 128), F32),
            pltpu.VMEM((CIN * (size_y + 8), size_z), F32),
            pltpu.VMEM((size_x + 6, CIN * (size_y + 8), size_z), BF16),
            pltpu.VMEM((n_samp, *piece1), F32),
            pltpu.VMEM((n_space, *piece2), F32),
            pltpu.VMEM((n_samp, *piece1), F32),
            pltpu.VMEM((n_space, *piece2), F32),
            pltpu.VMEM((n_space, *piece1), F32),
            pltpu.VMEM((n_samp, *piece2), F32),
            pltpu.VMEM(piece1, F32),
            pltpu.VMEM(piece2, F32),
            sides, sides, sides, sides, samp, samp, space, space,
            samp, samp, space, space, space, space, samp, samp,
        ],
        compiler_params=pltpu.CompilerParams(
            collective_id=0, has_side_effects=True, vmem_limit_bytes=48 * 2**20),
    )(volume, cotangent,
      filters_one.reshape(piece1), filters_two.reshape(piece2))
    return activation, out1.reshape(len1), out2.reshape(len2)


def solution(mesh):
    in_specs = (
        P(None, "space", "samp", None),
        P("samp"),
        P("space"),
        P(None, "space", "samp", None),
    )
    out_specs = (P(None, "space", "samp", None), P("samp"), P("space"))
    return jax.shard_map(
        functools.partial(on_device, mesh.shape["space"], mesh.shape["samp"]),
        mesh=mesh, in_specs=in_specs, out_specs=out_specs, check_vma=False,
    )
```
